512 devices in a mesh: grp: 16 (over z), tile: 32 (over x, y, core).
Axes of the slice: x: 4, y: 4, z: 16, core: 2. Of those that a mesh axis runs over, the one named last changes fastest.
Arguments:
- seg_stream: int32 [512, 512, 32], P(('grp', 'tile')), may hold values from 0 to 1023
- seg_voxel: int32 [512, 512, 32], P(('grp', 'tile')), may hold values from 0 to 127
- seg_bin: int32 [512, 512, 32], P(('grp', 'tile')), may hold values from 0 to 511
- seg_length: float32 [512, 512, 32], P(('grp', 'tile')), may hold values from 0.02 to 0.06
- seg_count: int32 [512, 512], P(('grp', 'tile')), may hold values from 6 to 32, as said below
- stream_weight: float32 [524288], P(('grp', 'tile')), may hold values from 0 to 2
- signal: bfloat16 [288, 65536], P(None, ('grp', 'tile')), may hold values from 0.19921875 to 2
- peak_bin: int32 [3, 65536], P(None, ('grp', 'tile')), may hold values from 0 to 511
- extra_weight: float32 [3, 65536], P(None, ('grp', 'tile')), may hold values from 0 to 1
- iso_weight: float32 [65536], P(('grp', 'tile')), may hold values from 0 to 1
- intra_kernel: float32 [288, 512], replicated, may hold values from 0 to 1
- extra_kernel: float32 [288, 512], replicated, may hold values from 0 to 1
- iso_kernel: float32 [288], replicated, may hold values from 0.3 to 1
- step_size: float32 [1], replicated, may hold values from 0.0010416667 to 0.004166667
Outputs:
- residual: float32 [288, 65536], P(None, ('grp', 'tile'))
- new_stream: float32 [524288], P(('grp', 'tile'))
- new_extra: float32 [3, 65536], P(None, ('grp', 'tile'))
- new_iso: float32 [65536], P(('grp', 'tile'))
The draws below stay inside these ranges and needn't reach their ends.
Inputs may be any that keep to these rules, and one draw needn't show every extreme that they name: `seg_count`: some tile receives 32 used slots from every streamline owner.
All inputs are finite; a program needn't handle non-finite values.
Results may differ from the reference program's by a relative error of at most 0.0003.
Values sent between devices are 32-bit elements; how exact they have to be, the bound alone decides.
No kernel may reach another device: no remote copies, remote signals or barrier semaphores. Data moves between devices by JAX's collectives and lax.ppermute only.
A program may use at most 64 MiB of HBM per device.

```python
import math
import jax
import jax.numpy as jnp
from jax import lax

ND = 288
NB = 512
NPEAK = 3
V_DEV = 128
S_DEV = 1024
OWNERS = 512
SEG_BLK = 32
VOX = 65536
STREAMS = 524288


def draw_seg_count(key, part):
    count_key = jax.random.fold_in(key, 11)
    owner_key = jax.random.fold_in(key, 12)
    counts = jax.random.randint(count_key, (OWNERS, OWNERS), max(1, SEG_BLK // 5), SEG_BLK + 1)
    full_owner = jax.random.randint(owner_key, (), 0, OWNERS)
    column = lax.broadcasted_iota(jnp.int32, (OWNERS, OWNERS), 1)
    return jnp.where(column == full_owner, SEG_BLK, counts).astype(jnp.int32)


def set_ends(entries, stream_key, least, largest):
    spot = [jax.random.randint(jax.random.fold_in(stream_key, axis), (), 0, length) for axis, length in enumerate(entries.shape)]
    widest = entries.shape.index(max(entries.shape))
    neighbour = spot[:widest] + [(spot[widest] + 1) % entries.shape[widest]] + spot[widest + 1:]
    return entries.at[tuple(spot)].set(least).at[tuple(neighbour)].set(largest)


def steps_of(own_key, shape, split, low, top_value):
    level, own = 1.0, jax.random.fold_in(own_key, 6)
    for position, parts in split:
        heights = jnp.exp(jax.random.uniform(jax.random.fold_in(own, position), (parts,), jnp.float32, low / len(split), top_value / len(split)))
        level = level * jnp.repeat(heights, shape[position] // parts).reshape([-1 if axis == position else 1 for axis in range(len(shape))])
    return level


def setup_inputs(seed: int = 0) -> dict:
    keys = jax.random.split(jax.random.key(seed), 15)
    return {
        "seg_stream": set_ends(jax.random.randint(keys[0], (OWNERS, OWNERS, SEG_BLK), 0, S_DEV), jax.random.fold_in(keys[0], 1), 0, S_DEV - 1).astype(jnp.int32),
        "seg_voxel": set_ends(jax.random.randint(keys[1], (OWNERS, OWNERS, SEG_BLK), 0, V_DEV), jax.random.fold_in(keys[1], 1), 0, V_DEV - 1).astype(jnp.int32),
        "seg_bin": set_ends(jax.random.randint(keys[2], (OWNERS, OWNERS, SEG_BLK), 0, NB), jax.random.fold_in(keys[2], 1), 0, NB - 1).astype(jnp.int32),
        "seg_length": jnp.clip(0.02 + 0.04 * jax.random.uniform(keys[3], (OWNERS, OWNERS, SEG_BLK), jnp.float32) ** steps_of(keys[3], (OWNERS, OWNERS, SEG_BLK), ((0, 512),), -0.2, 0.2), 0.02, 0.06),
        "seg_count": draw_seg_count(jax.random.fold_in(keys[14], 71), 0),
        "stream_weight": jnp.clip(2.0 * jax.random.uniform(keys[5], (STREAMS,), jnp.float32) ** steps_of(keys[5], (STREAMS,), ((0, 512),), -0.2, 0.2), 0.0, 2.0),
        "signal": jnp.clip(0.19921875 + 1.8007812 * jax.random.uniform(keys[6], (ND, VOX), jnp.float32) ** steps_of(keys[6], (ND, VOX), ((1, 512),), -0.2, 0.2), 0.19921875, 2.0).astype(jnp.bfloat16),
        "peak_bin": set_ends(jax.random.randint(keys[7], (NPEAK, VOX), 0, NB), jax.random.fold_in(keys[7], 1), 0, NB - 1).astype(jnp.int32),
        "extra_weight": jnp.clip(1.0 * jax.random.uniform(keys[8], (NPEAK, VOX), jnp.float32) ** steps_of(keys[8], (NPEAK, VOX), ((1, 512),), -0.2, 0.2), 0.0, 1.0),
        "iso_weight": jnp.clip(1.0 * jax.random.uniform(keys[9], (VOX,), jnp.float32) ** steps_of(keys[9], (VOX,), ((0, 512),), -0.2, 0.2), 0.0, 1.0),
        "intra_kernel": jnp.clip(jax.random.uniform(keys[10], (ND, NB), jnp.float32, 0.0, 1.0), 0.0, 1.0),
        "extra_kernel": jnp.clip(jax.random.uniform(keys[11], (ND, NB), jnp.float32, 0.0, 1.0), 0.0, 1.0),
        "iso_kernel": jnp.clip(jax.random.uniform(keys[12], (ND,), jnp.float32, 0.3, 1.0), 0.3, 1.0),
        "step_size": jnp.clip(jnp.exp(jax.random.uniform(keys[13], (1,), jnp.float32, math.log(0.0010416667), math.log(0.004166667))), 0.0010416667, 0.004166667),
    }


def reference(seg_stream, seg_voxel, seg_bin, seg_length, seg_count, stream_weight, signal, peak_bin, extra_weight, iso_weight, intra_kernel, extra_kernel, iso_kernel, step_size):
    slot_index = lax.broadcasted_iota(jnp.int32, (OWNERS, OWNERS, SEG_BLK), 2)
    live_mask = (slot_index < seg_count[:, :, None]).astype(jnp.float32)
    length_live = seg_length * live_mask
    first_ids = (lax.broadcasted_iota(jnp.int32, (OWNERS, OWNERS, SEG_BLK), 0) * S_DEV).astype(jnp.int32)
    global_stream = (first_ids + seg_stream).astype(jnp.int32)
    seg_value = stream_weight[global_stream] * length_live
    seg_keys = (seg_bin * V_DEV + seg_voxel).astype(jnp.int32)
    values_dest = jnp.swapaxes(seg_value, 0, 1)
    keys_dest = jnp.swapaxes(seg_keys, 0, 1)
    measured_all = signal.astype(jnp.float32).reshape(ND, OWNERS, V_DEV).transpose(1, 0, 2)
    peaks_all = peak_bin.reshape(NPEAK, OWNERS, V_DEV).transpose(1, 0, 2)
    extra_all = extra_weight.reshape(NPEAK, OWNERS, V_DEV).transpose(1, 0, 2)
    iso_all = iso_weight.reshape(OWNERS, V_DEV)
    step = step_size[0]
    high = lax.Precision.HIGHEST

    def one_owner(pieces):
        values, owner_keys, measured, peak_ids, extra_w, iso_w = pieces
        flat_keys = owner_keys.reshape(-1)
        fiber_map = jax.ops.segment_sum(values.reshape(-1), flat_keys, num_segments=NB * V_DEV).reshape(NB, V_DEV)
        bin_ids = lax.broadcasted_iota(jnp.int32, (1, NB, 1), 1)
        extra_map = jnp.sum(jnp.where(peak_ids[:, None, :] == bin_ids, extra_w[:, None, :], 0.0), axis=0)
        resid = (jnp.dot(intra_kernel, fiber_map, precision=high) + jnp.dot(extra_kernel, extra_map, precision=high)
                 + iso_kernel[:, None] * iso_w[None, :] - measured)
        intra_back = jnp.dot(intra_kernel.T, resid, precision=high)
        extra_back = jnp.dot(extra_kernel.T, resid, precision=high)
        seg_back = intra_back.reshape(-1)[flat_keys].reshape(owner_keys.shape)
        extra_grad = jnp.take_along_axis(extra_back, peak_ids, axis=0)
        iso_grad = jnp.dot(iso_kernel, resid, precision=high)
        new_extra_w = jnp.maximum(extra_w - step * extra_grad, 0.0)
        new_iso_w = jnp.maximum(iso_w - step * iso_grad, 0.0)
        return resid, seg_back, new_extra_w, new_iso_w

    resid_all, back_all, extra_new, iso_new = lax.map(one_owner, (values_dest, keys_dest, measured_all, peaks_all, extra_all, iso_all))
    residual = resid_all.transpose(1, 0, 2).reshape(ND, VOX)
    new_extra = extra_new.transpose(1, 0, 2).reshape(NPEAK, VOX)
    new_iso = iso_new.reshape(VOX)
    seg_back = jnp.swapaxes(back_all, 0, 1)
    stream_grad = jax.ops.segment_sum((seg_back * length_live).reshape(-1), global_stream.reshape(-1), num_segments=STREAMS)
    new_stream = jnp.maximum(stream_weight - step * stream_grad, 0.0)
    return residual, new_stream, new_extra, new_iso
```

```python
import jax
import jax.numpy as jnp
from jax import lax
from jax.experimental import pallas as pl
from jax.experimental.pallas import tpu as pltpu
from jax.sharding import PartitionSpec as P

LANES = 128
F32 = jnp.float32
BF16 = jnp.bfloat16
HIGH = lax.Precision.HIGHEST


def iota(shape, dim):
    return lax.broadcasted_iota(jnp.int32, shape, dim)


def split2(x):
    head = x.astype(BF16)
    return head, (x - head.astype(F32)).astype(BF16)


def dot(a, b, dims):
    return lax.dot_general(a, b, (dims, ((), ())), preferred_element_type=F32)


def pack_rows(ref, per_row, rows):
    parts = [ref[0, pl.ds(q, rows, stride=per_row), :] for q in range(per_row)]
    return jnp.concatenate(parts, axis=1)


def prepare_kernel(stream_ref, voxel_ref, bin_ref, length_ref, count_ref, weight_ref,
                   out_ref, stream_out_ref, length_out_ref, *, num_voxels):
    owners, block = stream_ref.shape[1], stream_ref.shape[2]
    per_row = LANES // block
    rows = owners // per_row
    groups = out_ref.shape[0]
    half = rows // groups
    picked = jnp.where(iota((rows, owners), 1) // per_row == iota((rows, owners), 0),
                       count_ref[...].astype(F32), 0.0).astype(BF16)
    spread = (iota((owners, LANES), 0) % per_row
              == iota((owners, LANES), 1) // block).astype(F32).astype(BF16)
    counts = dot(picked, spread, ((1,), (0,)))
    slot = (iota((rows, LANES), 1) % block).astype(F32)
    length = jnp.where(slot < counts, pack_rows(length_ref, per_row, rows), 0.0)
    stream = pack_rows(stream_ref, per_row, rows)
    keys = pack_rows(bin_ref, per_row, rows) * num_voxels + pack_rows(voxel_ref, per_row, rows)
    lane_id = stream % LANES
    row_id = stream // LANES
    weight = jnp.zeros((rows, LANES), F32)
    for r in range(weight_ref.shape[0]):
        table = jnp.broadcast_to(weight_ref[r:r + 1, :], (rows, LANES))
        found = jnp.take_along_axis(table, lane_id, axis=1)
        weight = jnp.where(row_id == r, found, weight)
    value = weight * length
    keys = keys.astype(F32)
    for g in range(groups):
        out_ref[g, :half, :] = value[g * half:(g + 1) * half, :]
        out_ref[g, half:, :] = keys[g * half:(g + 1) * half, :]
    stream_out_ref[...] = stream
    length_out_ref[...] = length


def regroup_kernel(in_ref, out_ref, *, block, arrays):
    groups = in_ref.shape[0]
    per_row = LANES // block
    tile_rows = in_ref.shape[1] // arrays
    group_rows = groups // per_row
    stride = per_row * arrays * group_rows
    lane_part = iota((tile_rows, LANES), 1) // block
    for k in range(arrays):
        for a in range(group_rows):
            x = [in_ref[a * per_row + b, k * tile_rows:(k + 1) * tile_rows, :] for b in range(per_row)]
            for q in range(per_row):
                y = None
                for b in range(per_row):
                    shift = (block * (b - q)) % LANES
                    moved = pltpu.roll(x[b], shift, axis=1) if shift else x[b]
                    y = moved if y is None else jnp.where(lane_part == b, moved, y)
                out_ref[pl.ds(q * arrays * group_rows + k * group_rows + a, tile_rows, stride=stride), :] = y


def ungroup_kernel(in_ref, out_ref, *, block):
    groups, tile_rows = out_ref.shape[0], out_ref.shape[1]
    per_row = LANES // block
    group_rows = groups // per_row
    stride = per_row * group_rows
    lane_part = iota((tile_rows, LANES), 1) // block
    for a in range(group_rows):
        x = [in_ref[pl.ds(q * group_rows + a, tile_rows, stride=stride), :] for q in range(per_row)]
        for b in range(per_row):
            y = None
            for q in range(per_row):
                shift = (block * (q - b)) % LANES
                moved = pltpu.roll(x[q], shift, axis=1) if shift else x[q]
                y = moved if y is None else jnp.where(lane_part == q, moved, y)
            out_ref[a * per_row + b, :, :] = y


def backdrop_kernel(signal_ref, peak_ref, extra_ref, iso_ref, kernel_ref, iso_kernel_ref, out_ref):
    num_bins = kernel_ref.shape[1]
    num_voxels = peak_ref.shape[1]
    bins = iota((num_bins, num_voxels), 0)
    extra_map = jnp.zeros((num_bins, num_voxels), F32)
    for k in range(peak_ref.shape[0]):
        extra_map += jnp.where(bins == peak_ref[k:k + 1, :], extra_ref[k:k + 1, :], 0.0)
    zeppelin = jnp.dot(kernel_ref[...], extra_map, precision=HIGH, preferred_element_type=F32)
    out_ref[...] = zeppelin + iso_kernel_ref[...] * iso_ref[...] - signal_ref[...].astype(F32)


def tile_kernel(arrived_ref, backdrop_ref, kernel_ref, residual_ref, back_ref, bins_ref,
                *, num_voxels, chunk):
    tiles = arrived_ref.shape[0]
    half = arrived_ref.shape[1] // 2
    num_bins = kernel_ref.shape[1]
    width = half * LANES
    bin_ids = iota((num_bins, LANES), 0)
    voxel_ids = iota((num_voxels, LANES), 0)

    def scatter(c, acc):
        picked = []
        for i in range(chunk):
            t = c * chunk + i
            for r in range(half):
                value = arrived_ref[t, r:r + 1, :]
                key = arrived_ref[t, half + r:half + r + 1, :].astype(jnp.int32)
                hot = (bin_ids == key // num_voxels).astype(F32).astype(BF16)
                bins_ref[c, :, (i * half + r) * LANES:(i * half + r + 1) * LANES] = hot
                spread = jnp.where(voxel_ids == key % num_voxels, value, 0.0)
                picked.append(jnp.concatenate(split2(spread), axis=0))
        return acc + dot(bins_ref[c], jnp.concatenate(picked, axis=1), ((1,), (1,)))

    acc = lax.fori_loop(0, tiles // chunk, scatter, jnp.zeros((num_bins, 2 * num_voxels), F32))
    fiber = acc[:, :num_voxels] + acc[:, num_voxels:]
    residual = jnp.dot(kernel_ref[...], fiber, precision=HIGH, preferred_element_type=F32)
    residual += backdrop_ref[...]
    residual_ref[...] = residual
    back = lax.dot_general(residual, kernel_ref[...], (((0,), (0,)), ((), ())),
                           precision=HIGH, preferred_element_type=F32)
    back = jnp.concatenate(split2(back), axis=0)

    def gather(c, carry):
        rows = dot(back, bins_ref[c], ((1,), (0,)))
        rows = rows[:num_voxels] + rows[num_voxels:]
        for i in range(chunk):
            t = c * chunk + i
            for r in range(half):
                key = arrived_ref[t, half + r:half + r + 1, :].astype(jnp.int32)
                at = (i * half + r) * LANES
                hit = jnp.where(voxel_ids == key % num_voxels, rows[:, at:at + LANES], 0.0)
                back_ref[t, r:r + 1, :] = jnp.sum(hit, axis=0, keepdims=True)
        return carry

    lax.fori_loop(0, tiles // chunk, gather, 0)


def extra_kernel_body(residual_ref, peak_ref, extra_ref, iso_ref, kernel_ref, iso_kernel_ref, step_ref,
                      new_extra_ref, new_iso_ref):
    num_bins = kernel_ref.shape[1]
    num_voxels = peak_ref.shape[1]
    step = step_ref[0]
    residual = residual_ref[...]
    back = lax.dot_general(kernel_ref[...], residual, (((0,), (0,)), ((), ())),
                           precision=HIGH, preferred_element_type=F32)
    bins = iota((num_bins, num_voxels), 0)
    for k in range(peak_ref.shape[0]):
        grad = jnp.sum(jnp.where(bins == peak_ref[k:k + 1, :], back, 0.0), axis=0, keepdims=True)
        new_extra_ref[k:k + 1, :] = jnp.maximum(extra_ref[k:k + 1, :] - step * grad, 0.0)
    grad = jnp.sum(iso_kernel_ref[...] * residual, axis=0, keepdims=True)
    new_iso_ref[...] = jnp.maximum(iso_ref[...] - step * grad, 0.0)


def stream_kernel(back_ref, length_ref, stream_ref, weight_ref, step_ref, out_ref, *, chunk):
    rows = length_ref.shape[0]
    side = 32
    ids = iota((side, LANES), 0)
    back = back_ref[...].reshape(rows, LANES)
    acc = jnp.zeros((side, 2 * side), F32)
    contrib = back * length_ref[...]
    stream = stream_ref[...]
    for c in range(rows // chunk):
        high, low = [], []
        for r in range(c * chunk, (c + 1) * chunk):
            s = stream[r:r + 1, :]
            high.append((ids == s // side).astype(F32).astype(BF16))
            spread = jnp.where(ids == s % side, contrib[r:r + 1, :], 0.0)
            low.append(jnp.concatenate(split2(spread), axis=0))
        acc += dot(jnp.concatenate(high, axis=1), jnp.concatenate(low, axis=1), ((1,), (1,)))
    grad = acc[:, :side] + acc[:, side:]
    per_row = LANES // side
    out_rows = out_ref.shape[0]
    lines = [jnp.concatenate([grad[per_row * r + q:per_row * r + q + 1, :] for q in range(per_row)], axis=1)
             for r in range(out_rows)]
    grad = jnp.concatenate(lines, axis=0)
    out_ref[...] = jnp.maximum(weight_ref[...] - step_ref[0] * grad, 0.0)


VMEM = pl.BlockSpec(memory_space=pltpu.VMEM)
SMEM = pl.BlockSpec(memory_space=pltpu.SMEM)


def call(kernel, out_shape, in_specs, name, scratch=(), limit=48):
    multi = isinstance(out_shape, (list, tuple))
    return pl.pallas_call(
        kernel,
        out_shape=out_shape,
        in_specs=in_specs,
        out_specs=[VMEM] * len(out_shape) if multi else VMEM,
        scratch_shapes=scratch,
        compiler_params=pltpu.CompilerParams(vmem_limit_bytes=limit * 1024 * 1024),
        name=name,
    )


def shape(dims, dtype=F32):
    return jax.ShapeDtypeStruct(dims, dtype)


def on_device(seg_stream, seg_voxel, seg_bin, seg_length, seg_count, stream_weight, signal, peak_bin,
              extra_weight, iso_weight, intra_kernel, extra_kernel, iso_kernel, step_size):
    groups = lax.axis_size("grp")
    tiles = lax.axis_size("tile")
    owners, block = seg_stream.shape[1:]
    num_dirs, num_bins = intra_kernel.shape
    num_voxels = signal.shape[1]
    num_streams = stream_weight.shape[0]
    rows = owners * block // LANES
    tile_rows = rows // groups
    group_rows = rows // tiles
    weight_rows = stream_weight.reshape(num_streams // LANES, LANES)
    iso_row = iso_weight.reshape(1, num_voxels)
    iso_column = iso_kernel.reshape(num_dirs, 1)

    outgoing, stream, length = call(
        lambda *refs: prepare_kernel(*refs, num_voxels=num_voxels),
        [shape((groups, 2 * tile_rows, LANES)), shape((rows, LANES), jnp.int32), shape((rows, LANES))],
        [VMEM] * 6, "prepare",
    )(seg_stream, seg_voxel, seg_bin, seg_length, seg_count, weight_rows)
    passing = lax.all_to_all(outgoing, "grp", split_axis=0, concat_axis=0, tiled=True)
    backdrop = call(backdrop_kernel, shape((num_dirs, num_voxels)), [VMEM] * 6, "backdrop")(
        signal, peak_bin, extra_weight, iso_row, extra_kernel, iso_column)
    regrouped = call(
        lambda *refs: regroup_kernel(*refs, block=block, arrays=2),
        shape((tiles * 2 * group_rows, LANES)), [VMEM], "regroup",
    )(passing)
    arrived = lax.all_to_all(regrouped.reshape(tiles, 2 * group_rows, LANES), "tile",
                             split_axis=0, concat_axis=0, tiled=True)
    chunk = 4
    residual, seg_back = call(
        lambda *refs: tile_kernel(*refs, num_voxels=num_voxels, chunk=chunk),
        [shape((num_dirs, num_voxels)), shape((tiles, group_rows, LANES))],
        [VMEM] * 3, "tile",
        scratch=[pltpu.VMEM((tiles // chunk, num_bins, chunk * group_rows * LANES), BF16)],
    )(arrived, backdrop, intra_kernel)
    returning = lax.all_to_all(seg_back, "tile", split_axis=0, concat_axis=0, tiled=True)
    new_extra, new_iso = call(
        extra_kernel_body, [shape(extra_weight.shape), shape((1, num_voxels))],
        [VMEM] * 6 + [SMEM], "extra",
    )(residual, peak_bin, extra_weight, iso_row, extra_kernel, iso_column, step_size)
    ungrouped = call(
        lambda *refs: ungroup_kernel(*refs, block=block),
        shape((groups, tile_rows, LANES)), [VMEM], "ungroup",
    )(returning.reshape(tiles * group_rows, LANES))
    returned = lax.all_to_all(ungrouped, "grp", split_axis=0, concat_axis=0, tiled=True)
    new_stream = call(
        lambda *refs: stream_kernel(*refs, chunk=16),
        shape(weight_rows.shape), [VMEM] * 4 + [SMEM], "streams",
    )(returned, length, stream, weight_rows, step_size)
    return (residual, new_stream.reshape(num_streams), new_extra, new_iso.reshape(num_voxels))


def solution(mesh):
    split = ("grp", "tile")
    return jax.shard_map(
        on_device,
        mesh=mesh,
        in_specs=(
            P(split, None, None),
            P(split, None, None),
            P(split, None, None),
            P(split, None, None),
            P(split, None),
            P(split),
            P(None, split),
            P(None, split),
            P(None, split),
            P(split),
            P(),
            P(),
            P(),
            P(),
        ),
        out_specs=(
            P(None, split),
            P(split),
            P(None, split),
            P(split),
        ),
        check_vma=False,
    )
```

```python
import jax
import jax.numpy as jnp
from jax import lax
from jax.experimental import pallas as pl
from jax.experimental.pallas import tpu as pltpu
from jax.sharding import Mesh, PartitionSpec as P

LANES = 128
CORES = 2
CHUNK = 64
F32 = jnp.float32
BF16 = jnp.bfloat16
I16 = jnp.int16
HIGH = lax.Precision.HIGHEST


def iota(shape, dim):
    return lax.broadcasted_iota(jnp.int32, shape, dim)


def split2(x):
    head = x.astype(BF16)
    return head, (x - head.astype(F32)).astype(BF16)


def dot(a, b, dims):
    return lax.dot_general(a, b, (dims, ((), ())), preferred_element_type=F32)


def roll(x, shift):
    shift = shift % LANES
    return pltpu.roll(x, shift, axis=1) if shift else x


def side_by_side(parts, width, offset=0):
    lane_part = iota(parts[0].shape, 1) // width
    out = None
    for i, part in enumerate(parts):
        moved = roll(part, width * i - offset)
        out = moved if out is None else jnp.where(lane_part == i, moved, out)
    return out


def live_length(length_ref, count_ref):
    length = length_ref[0]
    return jnp.where(iota(length.shape, 0) < count_ref[...], length, 0.0)


def turned(a, b):
    pad = jnp.zeros((LANES - 2 * a.shape[0], LANES), F32)
    return jnp.transpose(jnp.concatenate([a, b, pad], axis=0))


def prepare_kernel(stream_hbm, voxel_hbm, bin_hbm, length_hbm, count_hbm, weight_hbm,
                   out_ref, turned_ref, stream_ref, voxel_ref, bin_ref, length_ref, count_ref, weight_ref,
                   sems, *, num_voxels):
    copies = [
        pltpu.make_async_copy(source, target, sems.at[i])
        for i, (source, target) in enumerate((
            (stream_hbm, stream_ref), (weight_hbm, weight_ref), (count_hbm, count_ref),
            (length_hbm, length_ref), (bin_hbm, bin_ref), (voxel_hbm, voxel_ref)))
    ]
    for copy in copies:
        copy.start()
    for copy in copies:
        copy.wait()
    block, owners = stream_ref.shape[1:]
    length = live_length(length_ref, count_ref)
    keys = (bin_ref[0] * num_voxels + voxel_ref[0]).astype(F32)
    tables = [jnp.broadcast_to(weight_ref[r:r + 1, :], (block, LANES)) for r in range(weight_ref.shape[0])]
    for start in range(0, owners, LANES):
        stream = stream_ref[0, :, start:start + LANES]
        lane_id = stream % LANES
        row_id = stream // LANES
        weight = jnp.zeros((block, LANES), F32)
        for r, table in enumerate(tables):
            weight = jnp.where(row_id == r, jnp.take_along_axis(table, lane_id, axis=1), weight)
        turned_ref[start:start + LANES, :] = turned(
            weight * length[:, start:start + LANES], keys[:, start:start + LANES])
    chips = owners // CORES
    out_ref[...] = side_by_side(
        [turned_ref[pl.ds(core, chips, stride=CORES), :] for core in range(CORES)], 2 * block)


def slots_kernel(stream_ref, length_ref, count_ref, stream_out_ref, length_out_ref, *, tiles):
    block, owners = stream_ref.shape[1:]
    length = live_length(length_ref, count_ref)
    stream = stream_ref[0].astype(F32)
    per_row = LANES // block
    height = tiles // per_row
    for start in range(0, owners, LANES):
        both = turned(stream[:, start:start + LANES], length[:, start:start + LANES])
        for first in range(0, LANES, tiles):
            parts = [both[first + u * height:first + (u + 1) * height, :] for u in range(per_row)]
            row = (start + first) // tiles * height
            stream_out_ref[row:row + height, :] = side_by_side(parts, block).astype(jnp.int32)
            length_out_ref[row:row + height, :] = side_by_side(parts, block, block)


def backdrop_kernel(signal_ref, peak_ref, extra_ref, iso_ref, kernel_ref, iso_kernel_ref, intra_ref,
                    out_ref, parts_ref):
    num_bins = kernel_ref.shape[1]
    num_voxels = peak_ref.shape[1]
    bins = iota((num_bins, num_voxels), 0)
    extra_map = jnp.zeros((num_bins, num_voxels), F32)
    for k in range(peak_ref.shape[0]):
        extra_map += jnp.where(bins == peak_ref[k:k + 1, :], extra_ref[k:k + 1, :], 0.0)
    zeppelin = jnp.dot(kernel_ref[...], extra_map, precision=HIGH, preferred_element_type=F32)
    out_ref[...] = zeppelin + iso_kernel_ref[...] * iso_ref[...] - signal_ref[...].astype(F32)
    parts_ref[0], parts_ref[1] = split2(intra_ref[...])


def tile_kernel(own_ref, other_ref, backdrop_ref, parts_ref, core_ref, residual_ref, back_ref,
                value_ref, key_ref, found_ref, *, num_voxels, block, group_rows):
    chips = own_ref.shape[0]
    num_bins = parts_ref.shape[2]
    per_row = LANES // block
    rows = chips // per_row
    places = rows // group_rows
    chunks, chunk = key_ref.shape[:2]
    bin_ids = iota((num_bins, LANES), 0).astype(I16)
    voxel_ids = iota((num_voxels, LANES), 0).astype(I16)
    voxel_ids32 = iota((num_voxels, LANES), 0)
    one, zero = jnp.ones((), BF16), jnp.zeros((), BF16)

    for source, ref in enumerate((own_ref, other_ref)):
        mine = ref[...]
        mine = jnp.where(core_ref[0] == 0, mine, pltpu.roll(mine, LANES // CORES, axis=1))
        quarters = [mine[b * rows:(b + 1) * rows, :] for b in range(per_row)]
        value = side_by_side(quarters, block)
        key = side_by_side(quarters, block, block)
        for start in range(0, rows, chunk):
            value_ref[(source * rows + start) // chunk] = value[start:start + chunk]
            key_ref[(source * rows + start) // chunk] = key[start:start + chunk].astype(jnp.int32)

    def hots(c):
        return jnp.concatenate([
            jnp.where(bin_ids == (key_ref[c, i:i + 1, :] // num_voxels).astype(I16), one, zero)
            for i in range(chunk)], axis=1)

    def scatter(c, acc):
        spread = []
        for i in range(chunk):
            head, tail = split2(value_ref[c, i:i + 1, :])
            here = voxel_ids == (key_ref[c, i:i + 1, :] % num_voxels).astype(I16)
            spread.append(jnp.concatenate([jnp.where(here, head, zero), jnp.where(here, tail, zero)], axis=0))
        return acc + dot(hots(c), jnp.concatenate(spread, axis=1), ((1,), (1,)))

    acc = lax.fori_loop(0, chunks, scatter, jnp.zeros((num_bins, 2 * num_voxels), F32))
    fiber = jnp.concatenate(split2(acc[:, :num_voxels] + acc[:, num_voxels:]), axis=1)
    product = dot(parts_ref[0], fiber, ((1,), (0,))) + dot(parts_ref[1], fiber, ((1,), (0,)))
    residual = product[:, :num_voxels] + product[:, num_voxels:] + backdrop_ref[...]
    residual_ref[...] = residual
    turned_residual = jnp.concatenate(split2(jnp.transpose(residual)), axis=0)
    product = dot(turned_residual, parts_ref[0], ((1,), (0,))) + dot(turned_residual, parts_ref[1], ((1,), (0,)))
    back = jnp.concatenate(split2(product[:num_voxels] + product[num_voxels:]), axis=0)

    def gather(c, carry):
        found = dot(back, hots(c), ((1,), (0,)))
        found = found[:num_voxels] + found[num_voxels:]
        for i in range(chunk):
            hit = jnp.where(voxel_ids32 == key_ref[c, i:i + 1, :] % num_voxels,
                            found[:, i * LANES:(i + 1) * LANES], 0.0)
            found_ref[c, i:i + 1, :] = jnp.sum(hit, axis=0, keepdims=True)
        return carry

    lax.fori_loop(0, chunks, gather, 0)
    for source in range(CORES):
        source_core = core_ref[0] if source == 0 else 1 - core_ref[0]
        for a in range(group_rows):
            n = source * rows + a * places
            back_ref[pl.ds(source_core * group_rows + a, places, stride=CORES * group_rows), :] = (
                found_ref[n // chunk, n % chunk:n % chunk + places, :])


def ungroup_kernel(in_ref, out_ref, *, block):
    groups, height = out_ref.shape[0], out_ref.shape[1]
    per_row = LANES // block
    group_rows = groups // per_row
    for a in range(group_rows):
        parts = [in_ref[pl.ds(u * height * group_rows + a, height, stride=group_rows), :]
                 for u in range(per_row)]
        for b in range(per_row):
            out_ref[b * group_rows + a] = side_by_side([roll(part, -block * b) for part in parts], block)


def extra_kernel_body(residual_ref, peak_ref, extra_ref, iso_ref, kernel_ref, iso_kernel_ref, step_ref,
                      new_extra_ref, new_iso_ref):
    num_bins = kernel_ref.shape[1]
    num_voxels = peak_ref.shape[1]
    step = step_ref[0]
    residual = residual_ref[...]
    back = lax.dot_general(kernel_ref[...], residual, (((0,), (0,)), ((), ())),
                           precision=HIGH, preferred_element_type=F32)
    bins = iota((num_bins, num_voxels), 0)
    for k in range(peak_ref.shape[0]):
        grad = jnp.sum(jnp.where(bins == peak_ref[k:k + 1, :], back, 0.0), axis=0, keepdims=True)
        new_extra_ref[k:k + 1, :] = jnp.maximum(extra_ref[k:k + 1, :] - step * grad, 0.0)
    grad = jnp.sum(iso_kernel_ref[...] * residual, axis=0, keepdims=True)
    new_iso_ref[...] = jnp.maximum(iso_ref[...] - step * grad, 0.0)


def stream_kernel(back_ref, length_ref, stream_ref, weight_ref, step_ref, out_ref):
    rows = length_ref.shape[0]
    side = 32
    ids = iota((side, LANES), 0).astype(I16)
    one, zero = jnp.ones((), BF16), jnp.zeros((), BF16)
    contrib = back_ref[...].reshape(rows, LANES) * length_ref[...]
    stream = stream_ref[...]
    major, minor = stream // side, stream % side
    high, low = [], []
    for r in range(rows):
        high.append(jnp.where(ids == major[r:r + 1, :].astype(I16), one, zero))
        here = ids == minor[r:r + 1, :].astype(I16)
        head, tail = split2(contrib[r:r + 1, :])
        low.append(jnp.concatenate([jnp.where(here, head, zero), jnp.where(here, tail, zero)], axis=0))
    acc = dot(jnp.concatenate(high, axis=1), jnp.concatenate(low, axis=1), ((1,), (1,)))
    grad = acc[:, :side] + acc[:, side:]
    per_row = LANES // side
    lines = [jnp.concatenate([grad[per_row * r + q:per_row * r + q + 1, :] for q in range(per_row)], axis=1)
             for r in range(out_ref.shape[0])]
    grad = jnp.concatenate(lines, axis=0)
    out_ref[...] = jnp.maximum(weight_ref[...] - step_ref[0] * grad, 0.0)


VMEM = pl.BlockSpec(memory_space=pltpu.VMEM)
HBM = pl.BlockSpec(memory_space=pltpu.HBM)
SMEM = pl.BlockSpec(memory_space=pltpu.SMEM)


def call(kernel, out_shape, in_specs, name, scratch=(), limit=16):
    multi = isinstance(out_shape, (list, tuple))
    return pl.pallas_call(
        kernel,
        out_shape=out_shape,
        in_specs=in_specs,
        out_specs=[VMEM] * len(out_shape) if multi else VMEM,
        scratch_shapes=scratch,
        compiler_params=pltpu.CompilerParams(vmem_limit_bytes=limit * 1024 * 1024),
        name=name,
    )


def shape(dims, dtype=F32):
    return jax.ShapeDtypeStruct(dims, dtype)


def on_device(seg_stream, seg_voxel, seg_bin, seg_length, seg_count, stream_weight, signal, peak_bin,
              extra_weight, iso_weight, intra_kernel, extra_kernel, iso_kernel, step_size):
    groups = lax.axis_size("grp")
    tiles = lax.axis_size("place") * CORES
    owners, block = seg_stream.shape[1:]
    num_dirs, num_bins = intra_kernel.shape
    num_voxels = signal.shape[1]
    num_streams = stream_weight.shape[0]
    chips = owners // CORES
    rows = owners * block // LANES
    tile_rows = rows // groups
    group_rows = rows // tiles
    weight_rows = stream_weight.reshape(num_streams // LANES, LANES)
    iso_row = iso_weight.reshape(1, num_voxels)
    iso_column = iso_kernel.reshape(num_dirs, 1)
    core = lax.axis_index("core").astype(jnp.int32).reshape(1)
    by_slot = [jnp.swapaxes(x, 1, 2) for x in (seg_stream, seg_voxel, seg_bin, seg_length)]

    outgoing = call(
        lambda *refs: prepare_kernel(*refs, num_voxels=num_voxels),
        shape((chips, LANES)), [HBM] * 6, "prepare",
        scratch=[pltpu.VMEM((owners, LANES), F32)]
        + [pltpu.VMEM((1, block, owners), jnp.int32)] * 3
        + [pltpu.VMEM((1, block, owners), F32), pltpu.VMEM((1, owners), jnp.int32),
           pltpu.VMEM(weight_rows.shape, F32), pltpu.SemaphoreType.DMA((6,))],
    )(*(pltpu.with_memory_space_constraint(x, pltpu.HBM) for x in (*by_slot, seg_count, weight_rows)))
    own = lax.all_to_all(outgoing.reshape(chips, 1, LANES), ("grp", "place"),
                         split_axis=0, concat_axis=0, tiled=True).reshape(chips, LANES)
    stream, length = call(
        lambda *refs: slots_kernel(*refs, tiles=tiles),
        [shape((rows, LANES), jnp.int32), shape((rows, LANES))], [VMEM] * 3, "slots",
    )(by_slot[0], by_slot[3], seg_count)
    backdrop, parts = call(
        backdrop_kernel, [shape((num_dirs, num_voxels)), shape((2, num_dirs, num_bins), BF16)],
        [VMEM] * 7, "backdrop",
    )(signal, peak_bin, extra_weight, iso_row, extra_kernel, iso_column, intra_kernel)
    chunked = (rows // CHUNK, CHUNK, LANES)
    own, stream, length, backdrop, parts = lax.optimization_barrier((own, stream, length, backdrop, parts))
    other = lax.ppermute(own, "core", [(0, 1), (1, 0)])
    residual, seg_back = call(
        lambda *refs: tile_kernel(*refs, num_voxels=num_voxels, block=block, group_rows=group_rows),
        [shape((num_dirs, num_voxels)), shape((rows, LANES))], [VMEM] * 4 + [SMEM], "tile",
        scratch=[pltpu.VMEM(chunked, F32), pltpu.VMEM(chunked, jnp.int32), pltpu.VMEM(chunked, F32)],
        limit=32,
    )(own, other, backdrop, parts, core)
    returning = lax.all_to_all(seg_back.reshape(tiles, group_rows, LANES), ("place", "core"), split_axis=0, concat_axis=0, tiled=True)
    new_extra, new_iso = call(
        extra_kernel_body, [shape(extra_weight.shape), shape((1, num_voxels))],
        [VMEM] * 6 + [SMEM], "extra",
    )(residual, peak_bin, extra_weight, iso_row, extra_kernel, iso_column, step_size)
    ungrouped = call(
        lambda *refs: ungroup_kernel(*refs, block=block),
        shape((groups, tile_rows, LANES)), [VMEM], "ungroup",
    )(returning.reshape(tiles * group_rows, LANES))
    returned = lax.all_to_all(ungrouped, "grp", split_axis=0, concat_axis=0, tiled=True)
    new_stream = call(
        stream_kernel, shape(weight_rows.shape), [VMEM] * 4 + [SMEM], "streams",
    )(returned, length, stream, weight_rows, step_size)
    return (residual, new_stream.reshape(num_streams), new_extra, new_iso.reshape(num_voxels))


def solution(mesh):
    groups, tiles = mesh.devices.shape
    split = ("grp", "place", "core")
    return jax.shard_map(
        on_device,
        mesh=Mesh(mesh.devices.reshape(groups, tiles // CORES, CORES), split),
        in_specs=(
            P(split, None, None),
            P(split, None, None),
            P(split, None, None),
            P(split, None, None),
            P(split, None),
            P(split),
            P(None, split),
            P(None, split),
            P(None, split),
            P(split),
            P(),
            P(),
            P(),
            P(),
        ),
        out_specs=(
            P(None, split),
            P(split),
            P(None, split),
            P(split),
        ),
        check_vma=False,
    )
```

```python
import jax
import jax.numpy as jnp
from jax import lax
from jax.experimental import pallas as pl
from jax.experimental.pallas import tpu as pltpu
from jax.sharding import Mesh, PartitionSpec as P

LANES = 128
CORES = 2
F32 = jnp.float32
BF16 = jnp.bfloat16
I16 = jnp.int16
HIGH = lax.Precision.HIGHEST


def iota(shape, dim):
    return lax.broadcasted_iota(jnp.int32, shape, dim)


def split2(x):
    head = x.astype(BF16)
    return head, (x - head.astype(F32)).astype(BF16)


def dot(a, b, dims):
    return lax.dot_general(a, b, (dims, ((), ())), preferred_element_type=F32)


def roll(x, shift):
    shift = shift % LANES
    return pltpu.roll(x, shift, axis=1) if shift else x


def side_by_side(parts, width, offset=0):
    lane_part = iota(parts[0].shape, 1) // width
    out = None
    for i, part in enumerate(parts):
        moved = roll(part, width * i - offset)
        out = moved if out is None else jnp.where(lane_part == i, moved, out)
    return out


def live_length(length_ref, count_ref):
    length = length_ref[0]
    return jnp.where(iota(length.shape, 0) < count_ref[...], length, 0.0)


def turned(a, b):
    pad = jnp.zeros((LANES - 2 * a.shape[0], LANES), F32)
    return jnp.transpose(jnp.concatenate([a, b, pad], axis=0))


def prepare_kernel(stream_hbm, voxel_hbm, bin_hbm, length_hbm, count_hbm, weight_hbm,
                   out_ref, turned_ref, stream_ref, voxel_ref, bin_ref, length_ref, count_ref, weight_ref,
                   sems, *, num_voxels):
    copies = [
        pltpu.make_async_copy(source, target, sems.at[i])
        for i, (source, target) in enumerate((
            (stream_hbm, stream_ref), (weight_hbm, weight_ref), (count_hbm, count_ref),
            (length_hbm, length_ref), (bin_hbm, bin_ref), (voxel_hbm, voxel_ref)))
    ]
    for copy in copies:
        copy.start()
    for copy in copies:
        copy.wait()
    block, owners = stream_ref.shape[1:]
    length = live_length(length_ref, count_ref)
    keys = (bin_ref[0] * num_voxels + voxel_ref[0]).astype(F32)
    tables = [jnp.broadcast_to(weight_ref[r:r + 1, :], (block, LANES)) for r in range(weight_ref.shape[0])]
    for start in range(0, owners, LANES):
        stream = stream_ref[0, :, start:start + LANES]
        lane_id = stream % LANES
        row_id = stream // LANES
        weight = jnp.zeros((block, LANES), F32)
        for r, table in enumerate(tables):
            weight = jnp.where(row_id == r, jnp.take_along_axis(table, lane_id, axis=1), weight)
        turned_ref[start:start + LANES, :] = turned(
            weight * length[:, start:start + LANES], keys[:, start:start + LANES])
    chips = owners // CORES
    out_ref[...] = side_by_side(
        [turned_ref[pl.ds(core, chips, stride=CORES), :] for core in range(CORES)], 2 * block)


def slots_kernel(stream_ref, length_ref, count_ref, stream_out_ref, length_out_ref, *, tiles):
    block, owners = stream_ref.shape[1:]
    length = live_length(length_ref, count_ref)
    stream = stream_ref[0].astype(F32)
    per_row = LANES // block
    height = tiles // per_row
    for start in range(0, owners, LANES):
        both = turned(stream[:, start:start + LANES], length[:, start:start + LANES])
        for first in range(0, LANES, tiles):
            parts = [both[first + u * height:first + (u + 1) * height, :] for u in range(per_row)]
            row = (start + first) // tiles * height
            stream_out_ref[row:row + height, :] = side_by_side(parts, block).astype(jnp.int32)
            length_out_ref[row:row + height, :] = side_by_side(parts, block, block)


def backdrop_kernel(signal_ref, peak_ref, extra_ref, iso_ref, kernel_ref, iso_kernel_ref, intra_ref,
                    out_ref, parts_ref):
    num_bins = kernel_ref.shape[1]
    num_voxels = peak_ref.shape[1]
    bins = iota((num_bins, num_voxels), 0)
    extra_map = jnp.zeros((num_bins, num_voxels), F32)
    for k in range(peak_ref.shape[0]):
        extra_map += jnp.where(bins == peak_ref[k:k + 1, :], extra_ref[k:k + 1, :], 0.0)
    zeppelin = jnp.dot(kernel_ref[...], extra_map, precision=HIGH, preferred_element_type=F32)
    out_ref[...] = zeppelin + iso_kernel_ref[...] * iso_ref[...] - signal_ref[...].astype(F32)
    parts_ref[0], parts_ref[1] = split2(intra_ref[...])


def unpack(ref, core, block):
    mine = ref[...]
    mine = jnp.where(core == 0, mine, pltpu.roll(mine, LANES // CORES, axis=1))
    per_row = LANES // block
    rows = mine.shape[0] // per_row
    quarters = [mine[b * rows:(b + 1) * rows, :] for b in range(per_row)]
    return side_by_side(quarters, block), side_by_side(quarters, block, block).astype(jnp.int32)


def where_bin(bin_ids, key_row, num_voxels):
    return jnp.where(bin_ids == (key_row // num_voxels).astype(I16), jnp.ones((), BF16), jnp.zeros((), BF16))


def scatter(value_ref, key_ref, num_bins, num_voxels):
    zero = jnp.zeros((), BF16)
    bin_ids = iota((num_bins, LANES), 0).astype(I16)
    voxel_ids = iota((num_voxels, LANES), 0).astype(I16)
    hots, spread = [], []
    for n in range(key_ref.shape[0]):
        key = key_ref[n:n + 1, :]
        head, tail = split2(value_ref[n:n + 1, :])
        here = voxel_ids == (key % num_voxels).astype(I16)
        spread.append(jnp.concatenate([jnp.where(here, head, zero), jnp.where(here, tail, zero)], axis=0))
        hots.append(where_bin(bin_ids, key, num_voxels))
    return dot(jnp.concatenate(hots, axis=1), jnp.concatenate(spread, axis=1), ((1,), (1,)))


def own_kernel(own_ref, acc_ref, keys_ref, value_ref, *, num_voxels, block):
    value_ref[...], keys_ref[...] = unpack(own_ref, lax.axis_index("core"), block)
    acc_ref[...] = scatter(value_ref, keys_ref, acc_ref.shape[0], num_voxels)


def tile_kernel(other_ref, acc_ref, own_keys_ref, backdrop_ref, parts_ref, residual_ref, back_ref,
                value_ref, keys_ref, found_ref, *, num_voxels, block, group_rows):
    core = lax.axis_index("core")
    num_bins = parts_ref.shape[2]
    rows = keys_ref.shape[1]
    places = rows // group_rows
    keys_ref[0] = own_keys_ref[...]
    value_ref[...], keys_ref[1] = unpack(other_ref, core, block)
    acc = acc_ref[...] + scatter(value_ref, keys_ref.at[1], num_bins, num_voxels)
    fiber = jnp.concatenate(split2(acc[:, :num_voxels] + acc[:, num_voxels:]), axis=1)
    product = dot(parts_ref[0], fiber, ((1,), (0,))) + dot(parts_ref[1], fiber, ((1,), (0,)))
    residual = product[:, :num_voxels] + product[:, num_voxels:] + backdrop_ref[...]
    residual_ref[...] = residual
    turned_residual = jnp.concatenate(split2(jnp.transpose(residual)), axis=0)
    product = dot(turned_residual, parts_ref[0], ((1,), (0,))) + dot(turned_residual, parts_ref[1], ((1,), (0,)))
    back = jnp.concatenate(split2(product[:num_voxels] + product[num_voxels:]), axis=0)
    bin_ids = iota((num_bins, LANES), 0).astype(I16)
    voxel_ids = iota((num_voxels, LANES), 0)

    def gather(source, carry):
        hots = [where_bin(bin_ids, keys_ref[source, n:n + 1, :], num_voxels) for n in range(rows)]
        found = dot(back, jnp.concatenate(hots, axis=1), ((1,), (0,)))
        found = found[:num_voxels] + found[num_voxels:]
        for n in range(rows):
            hit = jnp.where(voxel_ids == keys_ref[source, n:n + 1, :] % num_voxels,
                            found[:, n * LANES:(n + 1) * LANES], 0.0)
            found_ref[n:n + 1, :] = jnp.sum(hit, axis=0, keepdims=True)
        source_core = jnp.where(source == 0, core, 1 - core)
        for a in range(group_rows):
            back_ref[pl.ds(source_core * group_rows + a, places, stride=CORES * group_rows), :] = (
                found_ref[a * places:(a + 1) * places, :])
        return carry

    lax.fori_loop(0, CORES, gather, 0)


def ungroup_kernel(in_ref, out_ref, *, block):
    groups, height = out_ref.shape[0], out_ref.shape[1]
    per_row = LANES // block
    group_rows = groups // per_row
    for a in range(group_rows):
        parts = [in_ref[pl.ds(u * height * group_rows + a, height, stride=group_rows), :]
                 for u in range(per_row)]
        for b in range(per_row):
            out_ref[b * group_rows + a] = side_by_side([roll(part, -block * b) for part in parts], block)


def extra_kernel_body(residual_ref, peak_ref, extra_ref, iso_ref, kernel_ref, iso_kernel_ref, step_ref,
                      new_extra_ref, new_iso_ref):
    num_bins = kernel_ref.shape[1]
    num_voxels = peak_ref.shape[1]
    step = step_ref[0]
    residual = residual_ref[...]
    back = lax.dot_general(kernel_ref[...], residual, (((0,), (0,)), ((), ())),
                           precision=HIGH, preferred_element_type=F32)
    bins = iota((num_bins, num_voxels), 0)
    for k in range(peak_ref.shape[0]):
        grad = jnp.sum(jnp.where(bins == peak_ref[k:k + 1, :], back, 0.0), axis=0, keepdims=True)
        new_extra_ref[k:k + 1, :] = jnp.maximum(extra_ref[k:k + 1, :] - step * grad, 0.0)
    grad = jnp.sum(iso_kernel_ref[...] * residual, axis=0, keepdims=True)
    new_iso_ref[...] = jnp.maximum(iso_ref[...] - step * grad, 0.0)


def stream_kernel(back_ref, length_ref, stream_ref, weight_ref, step_ref, out_ref):
    rows = length_ref.shape[0]
    side = 32
    ids = iota((side, LANES), 0).astype(I16)
    one, zero = jnp.ones((), BF16), jnp.zeros((), BF16)
    contrib = back_ref[...].reshape(rows, LANES) * length_ref[...]
    stream = stream_ref[...]
    major, minor = stream // side, stream % side
    high, low = [], []
    for r in range(rows):
        high.append(jnp.where(ids == major[r:r + 1, :].astype(I16), one, zero))
        here = ids == minor[r:r + 1, :].astype(I16)
        head, tail = split2(contrib[r:r + 1, :])
        low.append(jnp.concatenate([jnp.where(here, head, zero), jnp.where(here, tail, zero)], axis=0))
    acc = dot(jnp.concatenate(high, axis=1), jnp.concatenate(low, axis=1), ((1,), (1,)))
    grad = acc[:, :side] + acc[:, side:]
    per_row = LANES // side
    lines = [jnp.concatenate([grad[per_row * r + q:per_row * r + q + 1, :] for q in range(per_row)], axis=1)
             for r in range(out_ref.shape[0])]
    grad = jnp.concatenate(lines, axis=0)
    out_ref[...] = jnp.maximum(weight_ref[...] - step_ref[0] * grad, 0.0)


VMEM = pl.BlockSpec(memory_space=pltpu.VMEM)
HBM = pl.BlockSpec(memory_space=pltpu.HBM)
SMEM = pl.BlockSpec(memory_space=pltpu.SMEM)


def call(kernel, out_shape, in_specs, name, scratch=(), limit=16):
    multi = isinstance(out_shape, (list, tuple))
    return pl.pallas_call(
        kernel,
        out_shape=out_shape,
        in_specs=in_specs,
        out_specs=[VMEM] * len(out_shape) if multi else VMEM,
        scratch_shapes=scratch,
        compiler_params=pltpu.CompilerParams(vmem_limit_bytes=limit * 1024 * 1024),
        name=name,
    )


def shape(dims, dtype=F32):
    return jax.ShapeDtypeStruct(dims, dtype)


def on_device(seg_stream, seg_voxel, seg_bin, seg_length, seg_count, stream_weight, signal, peak_bin,
              extra_weight, iso_weight, intra_kernel, extra_kernel, iso_kernel, step_size):
    groups = lax.axis_size("grp")
    tiles = lax.axis_size("place") * CORES
    owners, block = seg_stream.shape[1:]
    num_dirs, num_bins = intra_kernel.shape
    num_voxels = signal.shape[1]
    num_streams = stream_weight.shape[0]
    chips = owners // CORES
    rows = owners * block // LANES
    tile_rows = rows // groups
    group_rows = rows // tiles
    weight_rows = stream_weight.reshape(num_streams // LANES, LANES)
    iso_row = iso_weight.reshape(1, num_voxels)
    iso_column = iso_kernel.reshape(num_dirs, 1)
    by_slot = [jnp.swapaxes(x, 1, 2) for x in (seg_stream, seg_voxel, seg_bin, seg_length)]

    outgoing = call(
        lambda *refs: prepare_kernel(*refs, num_voxels=num_voxels),
        shape((chips, LANES)), [HBM] * 6, "prepare",
        scratch=[pltpu.VMEM((owners, LANES), F32)]
        + [pltpu.VMEM((1, block, owners), jnp.int32)] * 3
        + [pltpu.VMEM((1, block, owners), F32), pltpu.VMEM((1, owners), jnp.int32),
           pltpu.VMEM(weight_rows.shape, F32), pltpu.SemaphoreType.DMA((6,))],
    )(*(pltpu.with_memory_space_constraint(x, pltpu.HBM) for x in (*by_slot, seg_count, weight_rows)))
    own = lax.all_to_all(outgoing.reshape(chips, 1, LANES), ("grp", "place"),
                         split_axis=0, concat_axis=0, tiled=True).reshape(chips, LANES)
    stream, length = call(
        lambda *refs: slots_kernel(*refs, tiles=tiles),
        [shape((rows, LANES), jnp.int32), shape((rows, LANES))], [VMEM] * 3, "slots",
    )(by_slot[0], by_slot[3], seg_count)
    backdrop, parts = call(
        backdrop_kernel, [shape((num_dirs, num_voxels)), shape((2, num_dirs, num_bins), BF16)],
        [VMEM] * 7, "backdrop",
    )(signal, peak_bin, extra_weight, iso_row, extra_kernel, iso_column, intra_kernel)
    own, stream, length, backdrop, parts = lax.optimization_barrier((own, stream, length, backdrop, parts))
    other = lax.ppermute(own, "core", [(0, 1), (1, 0)])
    own_rows = rows // CORES
    acc, own_keys = call(
        lambda *refs: own_kernel(*refs, num_voxels=num_voxels, block=block),
        [shape((num_bins, 2 * num_voxels)), shape((own_rows, LANES), jnp.int32)], [VMEM], "own",
        scratch=[pltpu.VMEM((own_rows, LANES), F32)], limit=24,
    )(own)
    residual, seg_back = call(
        lambda *refs: tile_kernel(*refs, num_voxels=num_voxels, block=block, group_rows=group_rows),
        [shape((num_dirs, num_voxels)), shape((rows, LANES))], [VMEM] * 5, "tile",
        scratch=[pltpu.VMEM((own_rows, LANES), F32), pltpu.VMEM((CORES, own_rows, LANES), jnp.int32),
                 pltpu.VMEM((own_rows, LANES), F32)],
        limit=32,
    )(other, acc, own_keys, backdrop, parts)
    returning = lax.all_to_all(seg_back.reshape(tiles, group_rows, LANES), ("place", "core"), split_axis=0, concat_axis=0, tiled=True)
    new_extra, new_iso = call(
        extra_kernel_body, [shape(extra_weight.shape), shape((1, num_voxels))],
        [VMEM] * 6 + [SMEM], "extra",
    )(residual, peak_bin, extra_weight, iso_row, extra_kernel, iso_column, step_size)
    ungrouped = call(
        lambda *refs: ungroup_kernel(*refs, block=block),
        shape((groups, tile_rows, LANES)), [VMEM], "ungroup",
    )(returning.reshape(tiles * group_rows, LANES))
    returned = lax.all_to_all(ungrouped, "grp", split_axis=0, concat_axis=0, tiled=True)
    new_stream = call(
        stream_kernel, shape(weight_rows.shape), [VMEM] * 4 + [SMEM], "streams",
    )(returned, length, stream, weight_rows, step_size)
    return (residual, new_stream.reshape(num_streams), new_extra, new_iso.reshape(num_voxels))


def solution(mesh):
    groups, tiles = mesh.devices.shape
    split = ("grp", "place", "core")
    return jax.shard_map(
        on_device,
        mesh=Mesh(mesh.devices.reshape(groups, tiles // CORES, CORES), split),
        in_specs=(
            P(split, None, None),
            P(split, None, None),
            P(split, None, None),
            P(split, None, None),
            P(split, None),
            P(split),
            P(None, split),
            P(None, split),
            P(None, split),
            P(split),
            P(),
            P(),
            P(),
            P(),
        ),
        out_specs=(
            P(None, split),
            P(split),
            P(None, split),
            P(split),
        ),
        check_vma=False,
    )
```

```python
import jax
import jax.numpy as jnp
from jax import lax
from jax.experimental import pallas as pl
from jax.experimental.pallas import tpu as pltpu
from jax.sharding import Mesh, PartitionSpec as P

LANES = 128
CORES = 2
F32 = jnp.float32
BF16 = jnp.bfloat16
I16 = jnp.int16


def iota(shape, dim):
    return lax.broadcasted_iota(jnp.int32, shape, dim)


def split2(x):
    head = x.astype(BF16)
    return head, (x - head.astype(F32)).astype(BF16)


def dot(a, b, dims):
    return lax.dot_general(a, b, (dims, ((), ())), preferred_element_type=F32)


def roll(x, shift):
    shift = shift % LANES
    return pltpu.roll(x, shift, axis=1) if shift else x


def side_by_side(parts, width, offset=0):
    lane_part = iota(parts[0].shape, 1) // width
    out = None
    for i, part in enumerate(parts):
        moved = roll(part, width * i - offset)
        out = moved if out is None else jnp.where(lane_part == i, moved, out)
    return out


def live_length(length_ref, count_ref):
    length = length_ref[0]
    return jnp.where(iota(length.shape, 0) < count_ref[...], length, 0.0)


def turned(a, b):
    pad = jnp.zeros((LANES - 2 * a.shape[0], LANES), F32)
    return jnp.transpose(jnp.concatenate([a, b, pad], axis=0))


def prepare_kernel(stream_hbm, voxel_hbm, bin_hbm, length_hbm, count_hbm, weight_hbm,
                   out_ref, turned_ref, stream_ref, voxel_ref, bin_ref, length_ref, count_ref, weight_ref,
                   sems, *, num_voxels):
    copies = [
        pltpu.make_async_copy(source, target, sems.at[i])
        for i, (source, target) in enumerate((
            (stream_hbm, stream_ref), (weight_hbm, weight_ref), (count_hbm, count_ref),
            (length_hbm, length_ref), (bin_hbm, bin_ref), (voxel_hbm, voxel_ref)))
    ]
    for copy in copies:
        copy.start()
    for copy in copies:
        copy.wait()
    block, owners = stream_ref.shape[1:]
    length = live_length(length_ref, count_ref)
    keys = (bin_ref[0] * num_voxels + voxel_ref[0]).astype(F32)
    tables = [jnp.broadcast_to(weight_ref[r:r + 1, :], (block, LANES)) for r in range(weight_ref.shape[0])]
    for start in range(0, owners, LANES):
        stream = stream_ref[0, :, start:start + LANES]
        lane_id = stream % LANES
        row_id = stream // LANES
        weight = jnp.zeros((block, LANES), F32)
        for r, table in enumerate(tables):
            weight = jnp.where(row_id == r, jnp.take_along_axis(table, lane_id, axis=1), weight)
        turned_ref[start:start + LANES, :] = turned(
            weight * length[:, start:start + LANES], keys[:, start:start + LANES])
    chips = owners // CORES
    out_ref[...] = side_by_side(
        [turned_ref[pl.ds(core, chips, stride=CORES), :] for core in range(CORES)], 2 * block)


def slots_kernel(stream_ref, length_ref, count_ref, stream_out_ref, length_out_ref, *, tiles):
    block, owners = stream_ref.shape[1:]
    length = live_length(length_ref, count_ref)
    stream = stream_ref[0].astype(F32)
    per_row = LANES // block
    height = tiles // per_row
    for start in range(0, owners, LANES):
        both = turned(stream[:, start:start + LANES], length[:, start:start + LANES])
        for first in range(0, LANES, tiles):
            parts = [both[first + u * height:first + (u + 1) * height, :] for u in range(per_row)]
            row = (start + first) // tiles * height
            stream_out_ref[row:row + height, :] = side_by_side(parts, block).astype(jnp.int32)
            length_out_ref[row:row + height, :] = side_by_side(parts, block, block)


def backdrop_kernel(signal_ref, peak_ref, extra_ref, iso_ref, kernel_ref, iso_kernel_ref, intra_ref,
                    out_ref, parts_ref, peak_kernel_ref):
    num_bins = kernel_ref.shape[1]
    num_voxels = peak_ref.shape[1]
    peaks = peak_ref.shape[0]
    bins = iota((num_bins, num_voxels), 0)
    hot = jnp.concatenate([(bins == peak_ref[k:k + 1, :]).astype(F32).astype(BF16) for k in range(peaks)], axis=1)
    head, rest = kernel_ref[...].astype(BF16), kernel_ref[...]
    middle, tail = split2(rest - head.astype(F32))
    columns = dot(head, hot, ((1,), (0,))) + dot(middle, hot, ((1,), (0,))) + dot(tail, hot, ((1,), (0,)))
    backdrop = iso_kernel_ref[...] * iso_ref[...] - signal_ref[...].astype(F32)
    for k in range(peaks):
        column = columns[:, k * num_voxels:(k + 1) * num_voxels]
        peak_kernel_ref[k] = column
        backdrop += column * extra_ref[k:k + 1, :]
    out_ref[...] = backdrop
    parts_ref[0], parts_ref[1] = split2(intra_ref[...])


def unpack(ref, core, block):
    mine = ref[...]
    mine = jnp.where(core == 0, mine, pltpu.roll(mine, LANES // CORES, axis=1))
    per_row = LANES // block
    rows = mine.shape[0] // per_row
    quarters = [mine[b * rows:(b + 1) * rows, :] for b in range(per_row)]
    return side_by_side(quarters, block), side_by_side(quarters, block, block).astype(jnp.int32)


def where_bin(bin_ids, key_row, num_voxels):
    return jnp.where(bin_ids == (key_row // num_voxels).astype(I16), jnp.ones((), BF16), jnp.zeros((), BF16))


def scatter(value_ref, key_ref, num_bins, num_voxels):
    zero = jnp.zeros((), BF16)
    bin_ids = iota((num_bins, LANES), 0).astype(I16)
    voxel_ids = iota((num_voxels, LANES), 0).astype(I16)
    hots, spread = [], []
    for n in range(key_ref.shape[0]):
        key = key_ref[n:n + 1, :]
        head, tail = split2(value_ref[n:n + 1, :])
        here = voxel_ids == (key % num_voxels).astype(I16)
        spread.append(jnp.concatenate([jnp.where(here, head, zero), jnp.where(here, tail, zero)], axis=0))
        hots.append(where_bin(bin_ids, key, num_voxels))
    return dot(jnp.concatenate(hots, axis=1), jnp.concatenate(spread, axis=1), ((1,), (1,)))


def own_kernel(own_ref, acc_ref, keys_ref, value_ref, *, num_voxels, block):
    value_ref[...], keys_ref[...] = unpack(own_ref, lax.axis_index("core"), block)
    acc_ref[...] = scatter(value_ref, keys_ref, acc_ref.shape[0], num_voxels)


def tile_kernel(other_ref, acc_ref, own_keys_ref, backdrop_ref, parts_ref, peak_kernel_ref, extra_ref,
                iso_ref, iso_kernel_ref, step_ref,
                residual_ref, back_ref, new_extra_ref, new_iso_ref,
                value_ref, keys_ref, found_ref, *, num_voxels, block, group_rows):
    core = lax.axis_index("core")
    num_bins = parts_ref.shape[2]
    rows = keys_ref.shape[1]
    places = rows // group_rows
    keys_ref[0] = own_keys_ref[...]
    value_ref[...], keys_ref[1] = unpack(other_ref, core, block)
    acc = acc_ref[...] + scatter(value_ref, keys_ref.at[1], num_bins, num_voxels)
    fiber = jnp.concatenate(split2(acc[:, :num_voxels] + acc[:, num_voxels:]), axis=1)
    product = dot(parts_ref[0], fiber, ((1,), (0,))) + dot(parts_ref[1], fiber, ((1,), (0,)))
    residual = product[:, :num_voxels] + product[:, num_voxels:] + backdrop_ref[...]
    residual_ref[...] = residual
    turned_residual = jnp.concatenate(split2(jnp.transpose(residual)), axis=0)
    product = dot(turned_residual, parts_ref[0], ((1,), (0,))) + dot(turned_residual, parts_ref[1], ((1,), (0,)))
    back = jnp.concatenate(split2(product[:num_voxels] + product[num_voxels:]), axis=0)

    step = step_ref[0]
    for k in range(peak_kernel_ref.shape[0]):
        grad = jnp.sum(peak_kernel_ref[k] * residual, axis=0, keepdims=True)
        new_extra_ref[k:k + 1, :] = jnp.maximum(extra_ref[k:k + 1, :] - step * grad, 0.0)
    grad = jnp.sum(iso_kernel_ref[...] * residual, axis=0, keepdims=True)
    new_iso_ref[...] = jnp.maximum(iso_ref[...] - step * grad, 0.0)

    bin_ids = iota((num_bins, LANES), 0).astype(I16)
    voxel_ids = iota((num_voxels, LANES), 0)

    def gather(source, carry):
        hots = [where_bin(bin_ids, keys_ref[source, n:n + 1, :], num_voxels) for n in range(rows)]
        found = dot(back, jnp.concatenate(hots, axis=1), ((1,), (0,)))
        found = found[:num_voxels] + found[num_voxels:]
        for n in range(rows):
            hit = jnp.where(voxel_ids == keys_ref[source, n:n + 1, :] % num_voxels,
                            found[:, n * LANES:(n + 1) * LANES], 0.0)
            found_ref[n:n + 1, :] = jnp.sum(hit, axis=0, keepdims=True)
        source_core = jnp.where(source == 0, core, 1 - core)
        for a in range(group_rows):
            back_ref[pl.ds(source_core * group_rows + a, places, stride=CORES * group_rows), :] = (
                found_ref[a * places:(a + 1) * places, :])
        return carry

    lax.fori_loop(0, CORES, gather, 0)


def ungroup_kernel(in_ref, out_ref, *, block):
    groups, height = out_ref.shape[0], out_ref.shape[1]
    per_row = LANES // block
    group_rows = groups // per_row
    for a in range(group_rows):
        parts = [in_ref[pl.ds(u * height * group_rows + a, height, stride=group_rows), :]
                 for u in range(per_row)]
        for b in range(per_row):
            out_ref[b * group_rows + a] = side_by_side([roll(part, -block * b) for part in parts], block)


def stream_kernel(back_ref, length_ref, stream_ref, weight_ref, step_ref, out_ref):
    rows = length_ref.shape[0]
    side = 32
    ids = iota((side, LANES), 0).astype(I16)
    one, zero = jnp.ones((), BF16), jnp.zeros((), BF16)
    contrib = back_ref[...].reshape(rows, LANES) * length_ref[...]
    stream = stream_ref[...]
    major, minor = stream // side, stream % side
    high, low = [], []
    for r in range(rows):
        high.append(jnp.where(ids == major[r:r + 1, :].astype(I16), one, zero))
        here = ids == minor[r:r + 1, :].astype(I16)
        head, tail = split2(contrib[r:r + 1, :])
        low.append(jnp.concatenate([jnp.where(here, head, zero), jnp.where(here, tail, zero)], axis=0))
    acc = dot(jnp.concatenate(high, axis=1), jnp.concatenate(low, axis=1), ((1,), (1,)))
    grad = acc[:, :side] + acc[:, side:]
    per_row = LANES // side
    lines = [jnp.concatenate([grad[per_row * r + q:per_row * r + q + 1, :] for q in range(per_row)], axis=1)
             for r in range(out_ref.shape[0])]
    grad = jnp.concatenate(lines, axis=0)
    out_ref[...] = jnp.maximum(weight_ref[...] - step_ref[0] * grad, 0.0)


VMEM = pl.BlockSpec(memory_space=pltpu.VMEM)
HBM = pl.BlockSpec(memory_space=pltpu.HBM)
SMEM = pl.BlockSpec(memory_space=pltpu.SMEM)


def call(kernel, out_shape, in_specs, name, scratch=(), limit=16):
    multi = isinstance(out_shape, (list, tuple))
    return pl.pallas_call(
        kernel,
        out_shape=out_shape,
        in_specs=in_specs,
        out_specs=[VMEM] * len(out_shape) if multi else VMEM,
        scratch_shapes=scratch,
        compiler_params=pltpu.CompilerParams(vmem_limit_bytes=limit * 1024 * 1024),
        name=name,
    )


def shape(dims, dtype=F32):
    return jax.ShapeDtypeStruct(dims, dtype)


def on_device(seg_stream, seg_voxel, seg_bin, seg_length, seg_count, stream_weight, signal, peak_bin,
              extra_weight, iso_weight, intra_kernel, extra_kernel, iso_kernel, step_size):
    groups = lax.axis_size("grp")
    tiles = lax.axis_size("place") * CORES
    owners, block = seg_stream.shape[1:]
    num_dirs, num_bins = intra_kernel.shape
    num_voxels = signal.shape[1]
    num_streams = stream_weight.shape[0]
    chips = owners // CORES
    rows = owners * block // LANES
    tile_rows = rows // groups
    group_rows = rows // tiles
    weight_rows = stream_weight.reshape(num_streams // LANES, LANES)
    iso_row = iso_weight.reshape(1, num_voxels)
    iso_column = iso_kernel.reshape(num_dirs, 1)
    by_slot = [jnp.swapaxes(x, 1, 2) for x in (seg_stream, seg_voxel, seg_bin, seg_length)]

    outgoing = call(
        lambda *refs: prepare_kernel(*refs, num_voxels=num_voxels),
        shape((chips, LANES)), [HBM] * 6, "prepare",
        scratch=[pltpu.VMEM((owners, LANES), F32)]
        + [pltpu.VMEM((1, block, owners), jnp.int32)] * 3
        + [pltpu.VMEM((1, block, owners), F32), pltpu.VMEM((1, owners), jnp.int32),
           pltpu.VMEM(weight_rows.shape, F32), pltpu.SemaphoreType.DMA((6,))],
    )(*(pltpu.with_memory_space_constraint(x, pltpu.HBM) for x in (*by_slot, seg_count, weight_rows)))
    own = lax.all_to_all(outgoing.reshape(chips, 1, LANES), ("grp", "place"),
                         split_axis=0, concat_axis=0, tiled=True).reshape(chips, LANES)
    stream, length = call(
        lambda *refs: slots_kernel(*refs, tiles=tiles),
        [shape((rows, LANES), jnp.int32), shape((rows, LANES))], [VMEM] * 3, "slots",
    )(by_slot[0], by_slot[3], seg_count)
    backdrop, parts, peak_kernel = call(
        backdrop_kernel,
        [shape((num_dirs, num_voxels)), shape((2, num_dirs, num_bins), BF16), shape((*peak_bin.shape[:1], num_dirs, num_voxels))],
        [VMEM] * 7, "backdrop",
    )(signal, peak_bin, extra_weight, iso_row, extra_kernel, iso_column, intra_kernel)
    own, stream, length, backdrop, parts, peak_kernel = lax.optimization_barrier(
        (own, stream, length, backdrop, parts, peak_kernel))
    other = lax.ppermute(own, "core", [(0, 1), (1, 0)])
    own_rows = rows // CORES
    acc, own_keys = call(
        lambda *refs: own_kernel(*refs, num_voxels=num_voxels, block=block),
        [shape((num_bins, 2 * num_voxels)), shape((own_rows, LANES), jnp.int32)], [VMEM], "own",
        scratch=[pltpu.VMEM((own_rows, LANES), F32)], limit=24,
    )(own)
    residual, seg_back, new_extra, new_iso = call(
        lambda *refs: tile_kernel(*refs, num_voxels=num_voxels, block=block, group_rows=group_rows),
        [shape((num_dirs, num_voxels)), shape((rows, LANES)), shape(extra_weight.shape), shape((1, num_voxels))],
        [VMEM] * 9 + [SMEM], "tile",
        scratch=[pltpu.VMEM((own_rows, LANES), F32), pltpu.VMEM((CORES, own_rows, LANES), jnp.int32),
                 pltpu.VMEM((own_rows, LANES), F32)],
        limit=32,
    )(other, acc, own_keys, backdrop, parts, peak_kernel, extra_weight, iso_row, iso_column, step_size)
    returning = lax.all_to_all(seg_back.reshape(tiles, group_rows, LANES), ("place", "core"), split_axis=0, concat_axis=0, tiled=True)
    ungrouped = call(
        lambda *refs: ungroup_kernel(*refs, block=block),
        shape((groups, tile_rows, LANES)), [VMEM], "ungroup",
    )(returning.reshape(tiles * group_rows, LANES))
    returned = lax.all_to_all(ungrouped, "grp", split_axis=0, concat_axis=0, tiled=True)
    new_stream = call(
        stream_kernel, shape(weight_rows.shape), [VMEM] * 4 + [SMEM], "streams",
    )(returned, length, stream, weight_rows, step_size)
    return (residual, new_stream.reshape(num_streams), new_extra, new_iso.reshape(num_voxels))


def solution(mesh):
    groups, tiles = mesh.devices.shape
    split = ("grp", "place", "core")
    return jax.shard_map(
        on_device,
        mesh=Mesh(mesh.devices.reshape(groups, tiles // CORES, CORES), split),
        in_specs=(
            P(split, None, None),
            P(split, None, None),
            P(split, None, None),
            P(split, None, None),
            P(split, None),
            P(split),
            P(None, split),
            P(None, split),
            P(None, split),
            P(split),
            P(),
            P(),
            P(),
            P(),
        ),
        out_specs=(
            P(None, split),
            P(split),
            P(None, split),
            P(split),
        ),
        check_vma=False,
    )
```

```python
import jax
import jax.numpy as jnp
from jax import lax
from jax.experimental import pallas as pl
from jax.experimental.pallas import tpu as pltpu
from jax.sharding import Mesh, PartitionSpec as P

LANES = 128
CORES = 2
F32 = jnp.float32
BF16 = jnp.bfloat16
I16 = jnp.int16


def iota(shape, dim):
    return lax.broadcasted_iota(jnp.int32, shape, dim)


def split2(x):
    head = x.astype(BF16)
    return head, (x - head.astype(F32)).astype(BF16)


def dot(a, b, dims):
    return lax.dot_general(a, b, (dims, ((), ())), preferred_element_type=F32)


def roll(x, shift):
    shift = shift % LANES
    return pltpu.roll(x, shift, axis=1) if shift else x


def side_by_side(parts, width, offset=0):
    lane_part = iota(parts[0].shape, 1) // width
    out = None
    for i, part in enumerate(parts):
        moved = roll(part, width * i - offset)
        out = moved if out is None else jnp.where(lane_part == i, moved, out)
    return out


def live_length(length_ref, count_ref):
    length = length_ref[0]
    return jnp.where(iota(length.shape, 0) < count_ref[...], length, 0.0)


def turned(a, b):
    pad = jnp.zeros((LANES - 2 * a.shape[0], LANES), F32)
    return jnp.transpose(jnp.concatenate([a, b, pad], axis=0))


def prepare_kernel(stream_hbm, voxel_hbm, bin_hbm, length_hbm, count_hbm, weight_hbm,
                   out_ref, turned_ref, stream_ref, voxel_ref, bin_ref, length_ref, count_ref, weight_ref,
                   sems, *, num_voxels):
    copies = [
        pltpu.make_async_copy(source, target, sems.at[i])
        for i, (source, target) in enumerate((
            (stream_hbm, stream_ref), (weight_hbm, weight_ref), (count_hbm, count_ref),
            (length_hbm, length_ref), (bin_hbm, bin_ref), (voxel_hbm, voxel_ref)))
    ]
    for copy in copies:
        copy.start()
    for copy in copies:
        copy.wait()
    block, owners = stream_ref.shape[1:]
    length = live_length(length_ref, count_ref)
    keys = (bin_ref[0] * num_voxels + voxel_ref[0]).astype(F32)
    tables = [jnp.broadcast_to(weight_ref[r:r + 1, :], (block, LANES)) for r in range(weight_ref.shape[0])]
    for start in range(0, owners, LANES):
        stream = stream_ref[0, :, start:start + LANES]
        lane_id = stream % LANES
        row_id = stream // LANES
        weight = jnp.zeros((block, LANES), F32)
        for r, table in enumerate(tables):
            weight = jnp.where(row_id == r, jnp.take_along_axis(table, lane_id, axis=1), weight)
        turned_ref[start:start + LANES, :] = turned(
            weight * length[:, start:start + LANES], keys[:, start:start + LANES])
    chips = owners // CORES
    out_ref[...] = side_by_side(
        [turned_ref[pl.ds(core, chips, stride=CORES), :] for core in range(CORES)], 2 * block)


def slots_kernel(stream_ref, length_ref, count_ref, stream_out_ref, length_out_ref, *, tiles):
    block, owners = stream_ref.shape[1:]
    length = live_length(length_ref, count_ref)
    stream = stream_ref[0].astype(F32)
    per_row = LANES // block
    height = tiles // per_row
    for start in range(0, owners, LANES):
        both = turned(stream[:, start:start + LANES], length[:, start:start + LANES])
        for first in range(0, LANES, tiles):
            parts = [both[first + u * height:first + (u + 1) * height, :] for u in range(per_row)]
            row = (start + first) // tiles * height
            stream_out_ref[row:row + height, :] = side_by_side(parts, block).astype(jnp.int32)
            length_out_ref[row:row + height, :] = side_by_side(parts, block, block)


def backdrop_kernel(signal_ref, peak_ref, extra_ref, iso_ref, kernel_ref, iso_kernel_ref, intra_ref,
                    step_ref, out_ref, parts_ref, peak_kernel_ref, step_row_ref):
    num_bins = kernel_ref.shape[1]
    num_voxels = peak_ref.shape[1]
    peaks = peak_ref.shape[0]
    bins = iota((num_bins, num_voxels), 0)
    hot = jnp.concatenate([(bins == peak_ref[k:k + 1, :]).astype(F32).astype(BF16) for k in range(peaks)], axis=1)
    head, rest = kernel_ref[...].astype(BF16), kernel_ref[...]
    middle, tail = split2(rest - head.astype(F32))
    columns = dot(head, hot, ((1,), (0,))) + dot(middle, hot, ((1,), (0,))) + dot(tail, hot, ((1,), (0,)))
    backdrop = iso_kernel_ref[...] * iso_ref[...] - signal_ref[...].astype(F32)
    for k in range(peaks):
        column = columns[:, k * num_voxels:(k + 1) * num_voxels]
        peak_kernel_ref[k] = column
        backdrop += column * extra_ref[k:k + 1, :]
    out_ref[...] = backdrop
    parts_ref[0], parts_ref[1] = split2(intra_ref[...])
    step_row_ref[...] = jnp.broadcast_to(step_ref[...], step_row_ref.shape)


def unpack(ref, core, block):
    mine = ref[...]
    mine = jnp.where(core == 0, mine, pltpu.roll(mine, LANES // CORES, axis=1))
    per_row = LANES // block
    rows = mine.shape[0] // per_row
    quarters = [mine[b * rows:(b + 1) * rows, :] for b in range(per_row)]
    return side_by_side(quarters, block), side_by_side(quarters, block, block).astype(jnp.int32)


def where_bin(bin_ids, key_row, num_voxels):
    return jnp.where(bin_ids == (key_row // num_voxels).astype(I16), jnp.ones((), BF16), jnp.zeros((), BF16))


def scatter(value_ref, key_ref, num_bins, num_voxels):
    zero = jnp.zeros((), BF16)
    bin_ids = iota((num_bins, LANES), 0).astype(I16)
    voxel_ids = iota((num_voxels, LANES), 0).astype(I16)
    hots, spread = [], []
    for n in range(key_ref.shape[0]):
        key = key_ref[n:n + 1, :]
        head, tail = split2(value_ref[n:n + 1, :])
        here = voxel_ids == (key % num_voxels).astype(I16)
        spread.append(jnp.concatenate([jnp.where(here, head, zero), jnp.where(here, tail, zero)], axis=0))
        hots.append(where_bin(bin_ids, key, num_voxels))
    return dot(jnp.concatenate(hots, axis=1), jnp.concatenate(spread, axis=1), ((1,), (1,)))


def own_kernel(own_ref, acc_ref, keys_ref, value_ref, *, num_voxels, block):
    value_ref[...], keys_ref[...] = unpack(own_ref, lax.axis_index("core"), block)
    acc_ref[...] = scatter(value_ref, keys_ref, acc_ref.shape[0], num_voxels)


def tile_kernel(other_ref, acc_ref, own_keys_ref, backdrop_ref, parts_ref, peak_kernel_ref, extra_ref,
                iso_ref, iso_kernel_ref, step_ref,
                residual_ref, back_ref, new_extra_ref, new_iso_ref,
                value_ref, keys_ref, found_ref, *, num_voxels, block, group_rows):
    core = lax.axis_index("core")
    num_bins = parts_ref.shape[2]
    rows = keys_ref.shape[1]
    places = rows // group_rows
    keys_ref[0] = own_keys_ref[...]
    value_ref[...], keys_ref[1] = unpack(other_ref, core, block)
    acc = acc_ref[...] + scatter(value_ref, keys_ref.at[1], num_bins, num_voxels)
    fiber = jnp.concatenate(split2(acc[:, :num_voxels] + acc[:, num_voxels:]), axis=1)
    product = dot(parts_ref[0], fiber, ((1,), (0,))) + dot(parts_ref[1], fiber, ((1,), (0,)))
    residual = product[:, :num_voxels] + product[:, num_voxels:] + backdrop_ref[...]
    residual_ref[...] = residual
    turned_residual = jnp.concatenate(split2(jnp.transpose(residual)), axis=0)
    product = dot(turned_residual, parts_ref[0], ((1,), (0,))) + dot(turned_residual, parts_ref[1], ((1,), (0,)))
    back = jnp.concatenate(split2(product[:num_voxels] + product[num_voxels:]), axis=0)

    step = step_ref[...]
    for k in range(peak_kernel_ref.shape[0]):
        grad = jnp.sum(peak_kernel_ref[k] * residual, axis=0, keepdims=True)
        new_extra_ref[k:k + 1, :] = jnp.maximum(extra_ref[k:k + 1, :] - step * grad, 0.0)
    grad = jnp.sum(iso_kernel_ref[...] * residual, axis=0, keepdims=True)
    new_iso_ref[...] = jnp.maximum(iso_ref[...] - step * grad, 0.0)

    bin_ids = iota((num_bins, LANES), 0).astype(I16)
    voxel_ids = iota((num_voxels, LANES), 0)

    def gather(source, carry):
        hots = [where_bin(bin_ids, keys_ref[source, n:n + 1, :], num_voxels) for n in range(rows)]
        found = dot(back, jnp.concatenate(hots, axis=1), ((1,), (0,)))
        found = found[:num_voxels] + found[num_voxels:]
        for n in range(rows):
            hit = jnp.where(voxel_ids == keys_ref[source, n:n + 1, :] % num_voxels,
                            found[:, n * LANES:(n + 1) * LANES], 0.0)
            found_ref[n:n + 1, :] = jnp.sum(hit, axis=0, keepdims=True)
        source_core = jnp.where(source == 0, core, 1 - core)
        for a in range(group_rows):
            back_ref[pl.ds(source_core * group_rows + a, places, stride=CORES * group_rows), :] = (
                found_ref[a * places:(a + 1) * places, :])
        return carry

    lax.fori_loop(0, CORES, gather, 0)


def ungroup_kernel(in_ref, out_ref, *, block):
    groups, height = out_ref.shape[0], out_ref.shape[1]
    per_row = LANES // block
    group_rows = groups // per_row
    for a in range(group_rows):
        parts = [in_ref[pl.ds(u * height * group_rows + a, height, stride=group_rows), :]
                 for u in range(per_row)]
        for b in range(per_row):
            out_ref[b * group_rows + a] = side_by_side([roll(part, -block * b) for part in parts], block)


def stream_kernel(back_ref, length_ref, stream_ref, weight_ref, step_ref, out_ref):
    rows = length_ref.shape[0]
    side = 32
    ids = iota((side, LANES), 0).astype(I16)
    one, zero = jnp.ones((), BF16), jnp.zeros((), BF16)
    contrib = back_ref[...].reshape(rows, LANES) * length_ref[...]
    stream = stream_ref[...]
    major, minor = stream // side, stream % side
    high, low = [], []
    for r in range(rows):
        high.append(jnp.where(ids == major[r:r + 1, :].astype(I16), one, zero))
        here = ids == minor[r:r + 1, :].astype(I16)
        head, tail = split2(contrib[r:r + 1, :])
        low.append(jnp.concatenate([jnp.where(here, head, zero), jnp.where(here, tail, zero)], axis=0))
    acc = dot(jnp.concatenate(high, axis=1), jnp.concatenate(low, axis=1), ((1,), (1,)))
    grad = acc[:, :side] + acc[:, side:]
    per_row = LANES // side
    lines = [jnp.concatenate([grad[per_row * r + q:per_row * r + q + 1, :] for q in range(per_row)], axis=1)
             for r in range(out_ref.shape[0])]
    grad = jnp.concatenate(lines, axis=0)
    out_ref[...] = jnp.maximum(weight_ref[...] - step_ref[...] * grad, 0.0)


VMEM = pl.BlockSpec(memory_space=pltpu.VMEM)
HBM = pl.BlockSpec(memory_space=pltpu.HBM)


def call(kernel, out_shape, in_specs, name, scratch=(), limit=16):
    multi = isinstance(out_shape, (list, tuple))
    return pl.pallas_call(
        kernel,
        out_shape=out_shape,
        in_specs=in_specs,
        out_specs=[VMEM] * len(out_shape) if multi else VMEM,
        scratch_shapes=scratch,
        compiler_params=pltpu.CompilerParams(vmem_limit_bytes=limit * 1024 * 1024),
        name=name,
    )


def shape(dims, dtype=F32):
    return jax.ShapeDtypeStruct(dims, dtype)


def on_device(seg_stream, seg_voxel, seg_bin, seg_length, seg_count, stream_weight, signal, peak_bin,
              extra_weight, iso_weight, intra_kernel, extra_kernel, iso_kernel, step_size):
    groups = lax.axis_size("grp")
    tiles = lax.axis_size("place") * CORES
    owners, block = seg_stream.shape[1:]
    num_dirs, num_bins = intra_kernel.shape
    num_voxels = signal.shape[1]
    num_streams = stream_weight.shape[0]
    chips = owners // CORES
    rows = owners * block // LANES
    tile_rows = rows // groups
    group_rows = rows // tiles
    weight_rows = stream_weight.reshape(num_streams // LANES, LANES)
    iso_row = iso_weight.reshape(1, num_voxels)
    step = step_size.reshape(1, 1)
    iso_column = iso_kernel.reshape(num_dirs, 1)
    by_slot = [jnp.swapaxes(x, 1, 2) for x in (seg_stream, seg_voxel, seg_bin, seg_length)]

    outgoing = call(
        lambda *refs: prepare_kernel(*refs, num_voxels=num_voxels),
        shape((chips, LANES)), [HBM] * 6, "prepare",
        scratch=[pltpu.VMEM((owners, LANES), F32)]
        + [pltpu.VMEM((1, block, owners), jnp.int32)] * 3
        + [pltpu.VMEM((1, block, owners), F32), pltpu.VMEM((1, owners), jnp.int32),
           pltpu.VMEM(weight_rows.shape, F32), pltpu.SemaphoreType.DMA((6,))],
    )(*(pltpu.with_memory_space_constraint(x, pltpu.HBM) for x in (*by_slot, seg_count, weight_rows)))
    own = lax.all_to_all(outgoing.reshape(chips, 1, LANES), ("grp", "place"),
                         split_axis=0, concat_axis=0, tiled=True).reshape(chips, LANES)
    stream, length = call(
        lambda *refs: slots_kernel(*refs, tiles=tiles),
        [shape((rows, LANES), jnp.int32), shape((rows, LANES))], [VMEM] * 3, "slots",
    )(by_slot[0], by_slot[3], seg_count)
    backdrop, parts, peak_kernel, step_row = call(
        backdrop_kernel,
        [shape((num_dirs, num_voxels)), shape((2, num_dirs, num_bins), BF16), shape((*peak_bin.shape[:1], num_dirs, num_voxels)), shape((1, LANES))],
        [VMEM] * 8, "backdrop",
    )(signal, peak_bin, extra_weight, iso_row, extra_kernel, iso_column, intra_kernel, step)
    own, stream, length, backdrop, parts, peak_kernel, step_row = lax.optimization_barrier(
        (own, stream, length, backdrop, parts, peak_kernel, step_row))
    other = lax.ppermute(own, "core", [(0, 1), (1, 0)])
    own_rows = rows // CORES
    acc, own_keys = call(
        lambda *refs: own_kernel(*refs, num_voxels=num_voxels, block=block),
        [shape((num_bins, 2 * num_voxels)), shape((own_rows, LANES), jnp.int32)], [VMEM], "own",
        scratch=[pltpu.VMEM((own_rows, LANES), F32)], limit=24,
    )(own)
    residual, seg_back, new_extra, new_iso = call(
        lambda *refs: tile_kernel(*refs, num_voxels=num_voxels, block=block, group_rows=group_rows),
        [shape((num_dirs, num_voxels)), shape((rows, LANES)), shape(extra_weight.shape), shape((1, num_voxels))],
        [VMEM] * 10, "tile",
        scratch=[pltpu.VMEM((own_rows, LANES), F32), pltpu.VMEM((CORES, own_rows, LANES), jnp.int32),
                 pltpu.VMEM((own_rows, LANES), F32)],
        limit=32,
    )(other, acc, own_keys, backdrop, parts, peak_kernel, extra_weight, iso_row, iso_column, step_row)
    returning = lax.all_to_all(seg_back.reshape(tiles, group_rows, LANES), ("place", "core"), split_axis=0, concat_axis=0, tiled=True)
    ungrouped = call(
        lambda *refs: ungroup_kernel(*refs, block=block),
        shape((groups, tile_rows, LANES)), [VMEM], "ungroup",
    )(returning.reshape(tiles * group_rows, LANES))
    returned = lax.all_to_all(ungrouped, "grp", split_axis=0, concat_axis=0, tiled=True)
    new_stream = call(
        stream_kernel, shape(weight_rows.shape), [VMEM] * 5, "streams",
    )(returned, length, stream, weight_rows, step_row)
    return (residual, new_stream.reshape(num_streams), new_extra, new_iso.reshape(num_voxels))


def solution(mesh):
    groups, tiles = mesh.devices.shape
    split = ("grp", "place", "core")
    return jax.shard_map(
        on_device,
        mesh=Mesh(mesh.devices.reshape(groups, tiles // CORES, CORES), split),
        in_specs=(
            P(split, None, None),
            P(split, None, None),
            P(split, None, None),
            P(split, None, None),
            P(split, None),
            P(split),
            P(None, split),
            P(None, split),
            P(None, split),
            P(split),
            P(),
            P(),
            P(),
            P(),
        ),
        out_specs=(
            P(None, split),
            P(split),
            P(None, split),
            P(split),
        ),
        check_vma=False,
    )
```

```python
import jax
import jax.numpy as jnp
from jax import lax
from jax.experimental import pallas as pl
from jax.experimental.pallas import tpu as pltpu
from jax.sharding import Mesh, PartitionSpec as P

LANES = 128
CORES = 2
F32 = jnp.float32
BF16 = jnp.bfloat16
I16 = jnp.int16


def iota(shape, dim):
    return lax.broadcasted_iota(jnp.int32, shape, dim)


def split2(x):
    head = x.astype(BF16)
    return head, (x - head.astype(F32)).astype(BF16)


def dot(a, b, dims):
    return lax.dot_general(a, b, (dims, ((), ())), preferred_element_type=F32)


def roll(x, shift):
    shift = shift % LANES
    return pltpu.roll(x, shift, axis=1) if shift else x


def side_by_side(parts, width, offset=0):
    lane_part = iota(parts[0].shape, 1) // width
    out = None
    for i, part in enumerate(parts):
        moved = roll(part, width * i - offset)
        out = moved if out is None else jnp.where(lane_part == i, moved, out)
    return out


def live_length(length_ref, count_ref):
    length = length_ref[0]
    return jnp.where(iota(length.shape, 0) < count_ref[...], length, 0.0)


def turned(a, b):
    pad = jnp.zeros((LANES - 2 * a.shape[0], LANES), F32)
    return jnp.transpose(jnp.concatenate([a, b, pad], axis=0))


def prepare_kernel(stream_hbm, voxel_hbm, bin_hbm, length_hbm, count_hbm, weight_hbm,
                   out_ref, turned_ref, stream_ref, voxel_ref, bin_ref, length_ref, count_ref, weight_ref,
                   sems, *, num_voxels):
    copies = [
        pltpu.make_async_copy(source, target, sems.at[i])
        for i, (source, target) in enumerate((
            (stream_hbm, stream_ref), (weight_hbm, weight_ref), (count_hbm, count_ref),
            (length_hbm, length_ref), (bin_hbm, bin_ref), (voxel_hbm, voxel_ref)))
    ]
    for copy in copies:
        copy.start()
    for copy in copies:
        copy.wait()
    block, owners = stream_ref.shape[1:]
    length = live_length(length_ref, count_ref)
    keys = (bin_ref[0] * num_voxels + voxel_ref[0]).astype(F32)
    tables = [jnp.broadcast_to(weight_ref[r:r + 1, :], (block, LANES)) for r in range(weight_ref.shape[0])]
    for start in range(0, owners, LANES):
        stream = stream_ref[0, :, start:start + LANES]
        lane_id = stream % LANES
        row_id = stream // LANES
        weight = jnp.zeros((block, LANES), F32)
        for r, table in enumerate(tables):
            weight = jnp.where(row_id == r, jnp.take_along_axis(table, lane_id, axis=1), weight)
        turned_ref[start:start + LANES, :] = turned(
            weight * length[:, start:start + LANES], keys[:, start:start + LANES])
    chips = owners // CORES
    out_ref[...] = side_by_side(
        [turned_ref[pl.ds(core, chips, stride=CORES), :] for core in range(CORES)], 2 * block)


def slots_kernel(stream_ref, length_ref, count_ref, stream_out_ref, length_out_ref, *, tiles):
    block, owners = stream_ref.shape[1:]
    length = live_length(length_ref, count_ref)
    stream = stream_ref[0].astype(F32)
    per_row = LANES // block
    height = tiles // per_row
    for start in range(0, owners, LANES):
        both = turned(stream[:, start:start + LANES], length[:, start:start + LANES])
        for first in range(0, LANES, tiles):
            parts = [both[first + u * height:first + (u + 1) * height, :] for u in range(per_row)]
            row = (start + first) // tiles * height
            stream_out_ref[row:row + height, :] = side_by_side(parts, block).astype(jnp.int32)
            length_out_ref[row:row + height, :] = side_by_side(parts, block, block)


def backdrop_kernel(signal_ref, peak_ref, extra_ref, iso_ref, kernel_ref, iso_kernel_ref, intra_ref,
                    step_ref, out_ref, parts_ref, peak_kernel_ref, step_row_ref):
    num_bins = kernel_ref.shape[1]
    num_voxels = peak_ref.shape[1]
    peaks = peak_ref.shape[0]
    bins = iota((num_bins, num_voxels), 0)
    hot = jnp.concatenate([(bins == peak_ref[k:k + 1, :]).astype(F32).astype(BF16) for k in range(peaks)], axis=1)
    head, rest = kernel_ref[...].astype(BF16), kernel_ref[...]
    middle, tail = split2(rest - head.astype(F32))
    columns = dot(head, hot, ((1,), (0,))) + dot(middle, hot, ((1,), (0,))) + dot(tail, hot, ((1,), (0,)))
    backdrop = iso_kernel_ref[...] * iso_ref[...] - signal_ref[...].astype(F32)
    for k in range(peaks):
        column = columns[:, k * num_voxels:(k + 1) * num_voxels]
        peak_kernel_ref[k] = column
        backdrop += column * extra_ref[k:k + 1, :]
    out_ref[...] = backdrop
    parts_ref[0], parts_ref[1] = split2(intra_ref[...])
    step_row_ref[...] = jnp.broadcast_to(step_ref[...], step_row_ref.shape)


def unpack(ref, core, block):
    mine = ref[...]
    mine = jnp.where(core == 0, mine, pltpu.roll(mine, LANES // CORES, axis=1))
    per_row = LANES // block
    rows = mine.shape[0] // per_row
    quarters = [mine[b * rows:(b + 1) * rows, :] for b in range(per_row)]
    return side_by_side(quarters, block), side_by_side(quarters, block, block).astype(jnp.int32)


def where_bin(bin_ids, key_row, num_voxels):
    return jnp.where(bin_ids == (key_row // num_voxels).astype(I16), jnp.ones((), BF16), jnp.zeros((), BF16))


def scatter(value_ref, key_ref, num_bins, num_voxels):
    zero = jnp.zeros((), BF16)
    bin_ids = iota((num_bins, LANES), 0).astype(I16)
    voxel_ids = iota((num_voxels, LANES), 0).astype(I16)
    hots, spread = [], []
    for n in range(key_ref.shape[0]):
        key = key_ref[n:n + 1, :]
        head, tail = split2(value_ref[n:n + 1, :])
        here = voxel_ids == (key % num_voxels).astype(I16)
        spread.append(jnp.concatenate([jnp.where(here, head, zero), jnp.where(here, tail, zero)], axis=0))
        hots.append(where_bin(bin_ids, key, num_voxels))
    return dot(jnp.concatenate(hots, axis=1), jnp.concatenate(spread, axis=1), ((1,), (1,)))


def own_kernel(own_ref, acc_ref, keys_ref, value_ref, *, num_voxels, block):
    value_ref[...], keys_ref[...] = unpack(own_ref, lax.axis_index("core"), block)
    acc_ref[...] = scatter(value_ref, keys_ref, acc_ref.shape[0], num_voxels)


def tile_kernel(other_ref, acc_ref, own_keys_ref, backdrop_ref, parts_ref, peak_kernel_ref, extra_ref,
                iso_ref, iso_kernel_ref, step_ref,
                back_ref, residual_hbm, new_extra_hbm, new_iso_hbm,
                value_ref, keys_ref, found_ref, residual_ref, new_extra_ref, new_iso_ref, sems, *, num_voxels, block, group_rows):
    core = lax.axis_index("core")
    num_bins = parts_ref.shape[2]
    rows = keys_ref.shape[1]
    places = rows // group_rows
    keys_ref[0] = own_keys_ref[...]
    value_ref[...], keys_ref[1] = unpack(other_ref, core, block)
    acc = acc_ref[...] + scatter(value_ref, keys_ref.at[1], num_bins, num_voxels)
    fiber = jnp.concatenate(split2(acc[:, :num_voxels] + acc[:, num_voxels:]), axis=1)
    product = dot(parts_ref[0], fiber, ((1,), (0,))) + dot(parts_ref[1], fiber, ((1,), (0,)))
    residual = product[:, :num_voxels] + product[:, num_voxels:] + backdrop_ref[...]
    residual_ref[...] = residual
    turned_residual = jnp.concatenate(split2(jnp.transpose(residual)), axis=0)
    product = dot(turned_residual, parts_ref[0], ((1,), (0,))) + dot(turned_residual, parts_ref[1], ((1,), (0,)))
    back = jnp.concatenate(split2(product[:num_voxels] + product[num_voxels:]), axis=0)

    step = step_ref[...]
    for k in range(peak_kernel_ref.shape[0]):
        grad = jnp.sum(peak_kernel_ref[k] * residual, axis=0, keepdims=True)
        new_extra_ref[k:k + 1, :] = jnp.maximum(extra_ref[k:k + 1, :] - step * grad, 0.0)
    grad = jnp.sum(iso_kernel_ref[...] * residual, axis=0, keepdims=True)
    new_iso_ref[...] = jnp.maximum(iso_ref[...] - step * grad, 0.0)
    results = [
        pltpu.make_async_copy(source, target, sems.at[i])
        for i, (source, target) in enumerate((
            (residual_ref, residual_hbm), (new_extra_ref, new_extra_hbm), (new_iso_ref, new_iso_hbm)))
    ]
    for copy in results:
        copy.start()

    bin_ids = iota((num_bins, LANES), 0).astype(I16)
    voxel_ids = iota((num_voxels, LANES), 0)

    def gather(source, carry):
        hots = [where_bin(bin_ids, keys_ref[source, n:n + 1, :], num_voxels) for n in range(rows)]
        found = dot(back, jnp.concatenate(hots, axis=1), ((1,), (0,)))
        found = found[:num_voxels] + found[num_voxels:]
        for n in range(rows):
            hit = jnp.where(voxel_ids == keys_ref[source, n:n + 1, :] % num_voxels,
                            found[:, n * LANES:(n + 1) * LANES], 0.0)
            found_ref[n:n + 1, :] = jnp.sum(hit, axis=0, keepdims=True)
        source_core = jnp.where(source == 0, core, 1 - core)
        for a in range(group_rows):
            back_ref[pl.ds(source_core * group_rows + a, places, stride=CORES * group_rows), :] = (
                found_ref[a * places:(a + 1) * places, :])
        return carry

    lax.fori_loop(0, CORES, gather, 0)
    for copy in results:
        copy.wait()


def ungroup_kernel(in_ref, out_ref, *, block):
    groups, height = out_ref.shape[0], out_ref.shape[1]
    per_row = LANES // block
    group_rows = groups // per_row
    for a in range(group_rows):
        parts = [in_ref[pl.ds(u * height * group_rows + a, height, stride=group_rows), :]
                 for u in range(per_row)]
        for b in range(per_row):
            out_ref[b * group_rows + a] = side_by_side([roll(part, -block * b) for part in parts], block)


def stream_kernel(back_ref, length_ref, stream_ref, weight_ref, step_ref, out_ref):
    rows = length_ref.shape[0]
    side = 32
    ids = iota((side, LANES), 0).astype(I16)
    one, zero = jnp.ones((), BF16), jnp.zeros((), BF16)
    contrib = back_ref[...].reshape(rows, LANES) * length_ref[...]
    stream = stream_ref[...]
    major, minor = stream // side, stream % side
    high, low = [], []
    for r in range(rows):
        high.append(jnp.where(ids == major[r:r + 1, :].astype(I16), one, zero))
        here = ids == minor[r:r + 1, :].astype(I16)
        head, tail = split2(contrib[r:r + 1, :])
        low.append(jnp.concatenate([jnp.where(here, head, zero), jnp.where(here, tail, zero)], axis=0))
    acc = dot(jnp.concatenate(high, axis=1), jnp.concatenate(low, axis=1), ((1,), (1,)))
    grad = acc[:, :side] + acc[:, side:]
    per_row = LANES // side
    lines = [jnp.concatenate([grad[per_row * r + q:per_row * r + q + 1, :] for q in range(per_row)], axis=1)
             for r in range(out_ref.shape[0])]
    grad = jnp.concatenate(lines, axis=0)
    out_ref[...] = jnp.maximum(weight_ref[...] - step_ref[...] * grad, 0.0)


VMEM = pl.BlockSpec(memory_space=pltpu.VMEM)
HBM = pl.BlockSpec(memory_space=pltpu.HBM)


def call(kernel, out_shape, in_specs, name, scratch=(), limit=16, out_specs=None):
    if out_specs is None:
        out_specs = [VMEM] * len(out_shape) if isinstance(out_shape, list) else VMEM
    return pl.pallas_call(
        kernel,
        out_shape=out_shape,
        in_specs=in_specs,
        out_specs=out_specs,
        scratch_shapes=scratch,
        compiler_params=pltpu.CompilerParams(vmem_limit_bytes=limit * 1024 * 1024),
        name=name,
    )


def shape(dims, dtype=F32):
    return jax.ShapeDtypeStruct(dims, dtype)


def on_device(seg_stream, seg_voxel, seg_bin, seg_length, seg_count, stream_weight, signal, peak_bin,
              extra_weight, iso_weight, intra_kernel, extra_kernel, iso_kernel, step_size):
    groups = lax.axis_size("grp")
    tiles = lax.axis_size("place") * CORES
    owners, block = seg_stream.shape[1:]
    num_dirs, num_bins = intra_kernel.shape
    num_voxels = signal.shape[1]
    num_streams = stream_weight.shape[0]
    chips = owners // CORES
    rows = owners * block // LANES
    tile_rows = rows // groups
    group_rows = rows // tiles
    weight_rows = stream_weight.reshape(num_streams // LANES, LANES)
    iso_row = iso_weight.reshape(1, num_voxels)
    step = step_size.reshape(1, 1)
    iso_column = iso_kernel.reshape(num_dirs, 1)
    by_slot = [jnp.swapaxes(x, 1, 2) for x in (seg_stream, seg_voxel, seg_bin, seg_length)]

    outgoing = call(
        lambda *refs: prepare_kernel(*refs, num_voxels=num_voxels),
        shape((chips, LANES)), [HBM] * 6, "prepare",
        scratch=[pltpu.VMEM((owners, LANES), F32)]
        + [pltpu.VMEM((1, block, owners), jnp.int32)] * 3
        + [pltpu.VMEM((1, block, owners), F32), pltpu.VMEM((1, owners), jnp.int32),
           pltpu.VMEM(weight_rows.shape, F32), pltpu.SemaphoreType.DMA((6,))],
    )(*(pltpu.with_memory_space_constraint(x, pltpu.HBM) for x in (*by_slot, seg_count, weight_rows)))
    own = lax.all_to_all(outgoing.reshape(chips, 1, LANES), ("grp", "place"),
                         split_axis=0, concat_axis=0, tiled=True).reshape(chips, LANES)
    stream, length = call(
        lambda *refs: slots_kernel(*refs, tiles=tiles),
        [shape((rows, LANES), jnp.int32), shape((rows, LANES))], [VMEM] * 3, "slots",
    )(by_slot[0], by_slot[3], seg_count)
    backdrop, parts, peak_kernel, step_row = call(
        backdrop_kernel,
        [shape((num_dirs, num_voxels)), shape((2, num_dirs, num_bins), BF16), shape((*peak_bin.shape[:1], num_dirs, num_voxels)), shape((1, LANES))],
        [VMEM] * 8, "backdrop",
    )(signal, peak_bin, extra_weight, iso_row, extra_kernel, iso_column, intra_kernel, step)
    own, stream, length, backdrop, parts, peak_kernel, step_row = lax.optimization_barrier(
        (own, stream, length, backdrop, parts, peak_kernel, step_row))
    other = lax.ppermute(own, "core", [(0, 1), (1, 0)])
    own_rows = rows // CORES
    acc, own_keys = call(
        lambda *refs: own_kernel(*refs, num_voxels=num_voxels, block=block),
        [shape((num_bins, 2 * num_voxels)), shape((own_rows, LANES), jnp.int32)], [VMEM], "own",
        scratch=[pltpu.VMEM((own_rows, LANES), F32)], limit=24,
    )(own)
    seg_back, residual, new_extra, new_iso = call(
        lambda *refs: tile_kernel(*refs, num_voxels=num_voxels, block=block, group_rows=group_rows),
        [shape((rows, LANES)), shape((num_dirs, num_voxels)), shape(extra_weight.shape), shape((1, num_voxels))],
        [VMEM] * 10, "tile", out_specs=[VMEM, HBM, HBM, HBM],
        scratch=[pltpu.VMEM((own_rows, LANES), F32), pltpu.VMEM((CORES, own_rows, LANES), jnp.int32),
                 pltpu.VMEM((own_rows, LANES), F32), pltpu.VMEM((num_dirs, num_voxels), F32),
                 pltpu.VMEM(extra_weight.shape, F32), pltpu.VMEM((1, num_voxels), F32),
                 pltpu.SemaphoreType.DMA((3,))],
        limit=32,
    )(other, acc, own_keys, backdrop, parts, peak_kernel, extra_weight, iso_row, iso_column, step_row)
    returning = lax.all_to_all(seg_back.reshape(tiles, group_rows, LANES), ("place", "core"), split_axis=0, concat_axis=0, tiled=True)
    ungrouped = call(
        lambda *refs: ungroup_kernel(*refs, block=block),
        shape((groups, tile_rows, LANES)), [VMEM], "ungroup",
    )(returning.reshape(tiles * group_rows, LANES))
    returned = lax.all_to_all(ungrouped, "grp", split_axis=0, concat_axis=0, tiled=True)
    new_stream = call(
        stream_kernel, shape(weight_rows.shape), [VMEM] * 5, "streams",
    )(returned, length, stream, weight_rows, step_row)
    return (residual, new_stream.reshape(num_streams), new_extra, new_iso.reshape(num_voxels))


def solution(mesh):
    groups, tiles = mesh.devices.shape
    split = ("grp", "place", "core")
    return jax.shard_map(
        on_device,
        mesh=Mesh(mesh.devices.reshape(groups, tiles // CORES, CORES), split),
        in_specs=(
            P(split, None, None),
            P(split, None, None),
            P(split, None, None),
            P(split, None, None),
            P(split, None),
            P(split),
            P(None, split),
            P(None, split),
            P(None, split),
            P(split),
            P(),
            P(),
            P(),
            P(),
        ),
        out_specs=(
            P(None, split),
            P(split),
            P(None, split),
            P(split),
        ),
        check_vma=False,
    )
```
